128 devices in a mesh: gx: 8 (over x_lo, z), gy: 16 (over x_hi, y, core).
Axes of the slice: x: 4 (x_hi: 2, x_lo: 2; x = x_hi * 2 + x_lo), y: 4, z: 4, core: 2. Of those that a mesh axis runs over, the one named last changes fastest.
Arguments:
- fields: float32 [14, 128, 256, 128], P(None, 'gx', 'gy'), may hold values from -0.5 to 3, as said below
- droplet_state: float32 [5, 1048576], P(None, ('gx', 'gy')), may hold values from -1 to 2, as said below
- droplet_cell: int32 [1048576], P(('gx', 'gy')), may hold values from 0 to 32767
- new_cell: int32 [1048576], P(('gx', 'gy')), may hold values from 0 to 32767
- migration_lists: int32 [512, 256], P(('gx', 'gy')), may hold values from 0 to 8191, as said below
- droplet_counts: int32 [128, 5], P(('gx', 'gy')), may hold values from 64 to 8192, as said below
Outputs:
- section_rate: float32 [14, 128, 256, 128], P(None, 'gx', 'gy')
- droplets_after: float32 [5, 1179648], P(None, ('gx', 'gy'))
- cells_after: int32 [1179648], P(('gx', 'gy'))
The draws below stay inside these ranges and needn't reach their ends.
Inputs may be any that keep to these rules, and one draw needn't show every extreme that they name: `fields`: channel 0 (density) lies in 0.8 to 1.6, channels 1 to 3 (momentum) in -0.5 to 0.5, channel 4 (total energy) in 1.2 to 3, channels 5 to 13 (species) in 0.02 to 0.3. `droplet_state`: row 0 (mass) lies in 0.2 to 2, row 1 (temperature) in 0.5 to 1.5, rows 2 to 4 (velocity) in -1 to 1. `droplet_counts`: column 0 of row d is the number of live droplets of device d, which fill slots 0 onward; some device is full with 8192. Column 1 + r is the number leaving in direction r, from 64 to 256; every device sends exactly 256 in some direction. `migration_lists`: row 4 d + r lists, in its first droplet_counts[d, 1 + r] entries, live slots of device d leaving in direction r; no slot appears twice among a device's four rows; the remaining entries are 0.
All inputs are finite; a program needn't handle non-finite values.
Results may differ from the reference program's by a relative error of at most 0.0003.
Values sent between devices are 32-bit elements; how exact they have to be, the bound alone decides.
A program may use at most 192 MiB of HBM per device.

```python
import jax
import jax.numpy as jnp
from jax import lax

CX = 16
CY = 16
NZ = 128
P_DEV = 8192
CAP = 256
NX = 128
NY = 256
N_GX = 8
N_GY = 16
DEVICES = 128


def draw_fields(key, part):
    subkeys = jax.random.split(key, 4)
    shape = (NX, NY, NZ)
    density = jax.random.uniform(subkeys[0], shape, minval=0.8, maxval=1.6)
    momentum = jax.random.uniform(subkeys[1], (3,) + shape, minval=-0.5, maxval=0.5)
    energy = jax.random.uniform(subkeys[2], shape, minval=1.2, maxval=3.0)
    species = jax.random.uniform(subkeys[3], (9,) + shape, minval=0.02, maxval=0.3)
    return jnp.concatenate([density[None], momentum, energy[None], species], 0).astype(jnp.float32)


def draw_droplet_state(key, part):
    subkeys = jax.random.split(key, 3)
    total_slots = DEVICES * P_DEV
    droplet_mass = 0.2 * jnp.exp(jnp.log(10.0) * jax.random.uniform(subkeys[0], (1, total_slots)))
    temper = jax.random.uniform(subkeys[1], (1, total_slots), minval=0.5, maxval=1.5)
    velocity = jax.random.uniform(subkeys[2], (3, total_slots), minval=-1.0, maxval=1.0)
    return jnp.concatenate([droplet_mass, temper, velocity], 0).astype(jnp.float32)


def plan_droplets(key):
    base = jax.random.fold_in(key, 11)
    subkeys = jax.random.split(base, 5)
    device_ids = jnp.arange(DEVICES, dtype=jnp.int32)
    halvings = jax.random.randint(subkeys[0], (DEVICES,), 0, 4)
    full_device = jax.random.randint(subkeys[1], (), 0, DEVICES)
    live = jnp.where(device_ids == full_device, P_DEV, jnp.right_shift(jnp.int32(P_DEV), halvings.astype(jnp.int32)))
    sent = jax.random.randint(subkeys[2], (DEVICES, 4), CAP // 4, CAP + 1)
    full_direction = jax.random.randint(subkeys[3], (DEVICES,), 0, 4)
    directions = jnp.arange(4, dtype=jnp.int32)[None, :]
    sent = jnp.where(directions == full_direction[:, None], CAP, sent)
    least_direction = (full_direction[0] + 1) % 4
    sent = jnp.where((device_ids[:, None] == 0) & (directions == least_direction), CAP // 4, sent)

    def pick(device_key, live_count, sends):
        order = jax.random.permutation(device_key, P_DEV).astype(jnp.int32)
        positions = jnp.arange(P_DEV, dtype=jnp.int32)
        sort_keys = jnp.where(order < live_count, positions, P_DEV + positions)
        chosen = order[jnp.argsort(sort_keys)][:4 * CAP].reshape(4, CAP)
        return jnp.where(jnp.arange(CAP, dtype=jnp.int32)[None, :] < sends[:, None], chosen, 0)
    lists = jax.vmap(pick)(jax.random.split(subkeys[4], DEVICES), live, sent)
    counts = jnp.concatenate([live[:, None], sent], 1).astype(jnp.int32)
    return (counts, lists.reshape(DEVICES * 4, CAP).astype(jnp.int32))


def draw_droplet_counts(key, part):
    return plan_droplets(key)[0]


def draw_migration_lists(key, part):
    return plan_droplets(key)[1]


def plant(values, key, smallest, largest):
    dims = values.shape
    index_at = [jax.random.randint(jax.random.fold_in(key, axis), (), 0, dims[axis]) for axis in range(len(dims))]
    values = values.at[tuple(index_at)].set(smallest)
    longest = dims.index(max(dims))
    index_at[longest] = (index_at[longest] + 1) % dims[longest]
    return values.at[tuple(index_at)].set(largest)


def setup_inputs(seed: int = 0) -> dict:
    splits = jax.random.split(jax.random.key(seed), 7)
    fields = draw_fields(jax.random.fold_in(splits[6], 71), 0)
    droplet_state = draw_droplet_state(jax.random.fold_in(splits[6], 71), 0)
    droplet_cell = plant(jax.random.randint(splits[2], (DEVICES * P_DEV,), 0, CX * CY * NZ), jax.random.fold_in(splits[2], 1), 0, (CX * CY * NZ) - 1).astype(jnp.int32)
    new_cell = plant(jax.random.randint(splits[3], (DEVICES * P_DEV,), 0, CX * CY * NZ), jax.random.fold_in(splits[3], 1), 0, (CX * CY * NZ) - 1).astype(jnp.int32)
    migration_lists = draw_migration_lists(jax.random.fold_in(splits[6], 71), 0)
    droplet_counts = draw_droplet_counts(jax.random.fold_in(splits[6], 71), 0)
    return dict(fields=fields, droplet_state=droplet_state, droplet_cell=droplet_cell, new_cell=new_cell, migration_lists=migration_lists, droplet_counts=droplet_counts)


STENCIL = (0.8, -0.2, 4.0 / 105.0, -1.0 / 280.0)
INV_SPACING = 2.0
GAS_FACTOR = 0.4
RATE_CONST = 20.0
ACTIVATION = 2.0
REACTION_SHARES = (0.0, 0.0, 0.0, 0.0, 1.5, -1.0, -2.0, 1.5, 1.5, 0.0, 0.0, 0.0, 0.0, 0.0)
EVAP_RATE = 0.5
DRAG_RATE = 0.8
HEAT_RATE = 0.6
LATENT_HEAT = 0.3
STEP_SIZE = 0.05


def primitives(block):
    density = block[0]
    velocity = (block[1] / density, block[2] / density, block[3] / density)
    kinetic = 0.5 * (block[1] * block[1] + block[2] * block[2] + block[3] * block[3]) / density
    temper = (block[4] - kinetic) / density
    pressure = GAS_FACTOR * density * temper
    return density, velocity, temper, pressure


def periodic(flux, dim):
    total = jnp.zeros_like(flux)
    for offset, weight in enumerate(STENCIL):
        total = total + weight * (jnp.roll(flux, -(offset + 1), dim) - jnp.roll(flux, offset + 1, dim))
    return INV_SPACING * total


def droplet_terms(gas, state):
    density, velocity, temper, pressure = primitives(gas)
    fuel_share = gas[5] / density
    droplet_mass = state[0]
    drop_temp = state[1]
    size = jnp.cbrt(droplet_mass)
    evap = EVAP_RATE * size * jnp.log1p(temper / (1.0 + fuel_share))
    drag = [DRAG_RATE * size * (velocity[spatial] - state[2 + spatial]) for spatial in range(3)]
    heat = HEAT_RATE * size * (temper - drop_temp)
    sources = jnp.stack([evap,
                         evap * state[2] - drag[0],
                         evap * state[3] - drag[1],
                         evap * state[4] - drag[2],
                         evap * drop_temp - heat,
                         evap])
    new_state = jnp.stack([droplet_mass - STEP_SIZE * evap,
                           drop_temp + STEP_SIZE * (heat - LATENT_HEAT * evap) / droplet_mass,
                           state[2] + STEP_SIZE * drag[0] / droplet_mass,
                           state[3] + STEP_SIZE * drag[1] / droplet_mass,
                           state[4] + STEP_SIZE * drag[2] / droplet_mass])
    return sources, new_state


def reference(fields, droplet_state, droplet_cell, new_cell, migration_lists, droplet_counts):
    n_fields = fields.shape[0]
    devices = N_GX * N_GY
    slots = P_DEV
    capacity = CAP
    density, velocity, temper, pressure = primitives(fields)
    rate = RATE_CONST * fields[5] * fields[6] / density * jnp.exp(-ACTIVATION / temper)
    shares = jnp.array(REACTION_SHARES, dtype=fields.dtype)

    def one_field(field_index):
        field = lax.dynamic_index_in_dim(fields, field_index, 0, keepdims=False)
        total = jnp.zeros_like(field)
        for spatial in range(3):
            first = (field_index == spatial + 1).astype(fields.dtype)
            fourth = (field_index == 4).astype(fields.dtype)
            flux = velocity[spatial] * field + pressure * first + pressure * velocity[spatial] * fourth
            total = total + periodic(flux, spatial)
        share = lax.dynamic_index_in_dim(shares, field_index, 0, keepdims=False)
        return -total + share * rate

    gas_rate = lax.map(one_field, jnp.arange(n_fields, dtype=jnp.int32))

    every_slot = jnp.arange(devices * slots, dtype=jnp.int32)
    owner = every_slot // slots
    slot_index = every_slot % slots
    live = slot_index < droplet_counts[owner, 0]
    row_x = owner // N_GY
    row_y = owner % N_GY
    local_x = droplet_cell // (CY * NZ)
    local_y = (droplet_cell // NZ) % CY
    local_z = droplet_cell % NZ
    flat_cell = ((row_x * CX + local_x) * NY + row_y * CY + local_y) * NZ + local_z
    gas = jnp.take(fields.reshape(n_fields, -1), flat_cell, axis=1)
    sources, new_state = droplet_terms(gas, droplet_state)
    sources = jnp.where(live[None], sources, 0.0)
    cell_total = NX * NY * NZ
    deposit = jax.vmap(lambda source_row: jax.ops.segment_sum(source_row, flat_cell, num_segments=cell_total))(sources)
    section_rate = gas_rate.at[:6].add(deposit.reshape(6, NX, NY, NZ))

    lists = migration_lists.reshape(devices, 4, capacity)
    sent = droplet_counts[:, 1:5]
    valid = jnp.arange(capacity, dtype=jnp.int32)[None, None, :] < sent[:, :, None]
    picked = jnp.arange(devices, dtype=jnp.int32)[:, None, None] * slots + lists
    send_state = jnp.where(valid[None], jnp.take(new_state, picked, axis=1), 0.0)
    send_cell = jnp.where(valid, jnp.take(new_cell, picked), -1)
    departed = jnp.zeros((devices * slots,), jnp.int32).at[picked.reshape(-1)].add(valid.reshape(-1).astype(jnp.int32))
    staying = live & (departed == 0)
    own_state = jnp.where(staying[None], new_state, 0.0).reshape(5, devices, slots)
    own_cell = jnp.where(staying, new_cell, -1).reshape(devices, slots)
    device_ids = jnp.arange(devices, dtype=jnp.int32)
    dev_x = device_ids // N_GY
    dev_y = device_ids % N_GY
    sources_of = [((dev_x - 1) % N_GX) * N_GY + dev_y,
                  ((dev_x + 1) % N_GX) * N_GY + dev_y,
                  dev_x * N_GY + (dev_y - 1) % N_GY,
                  dev_x * N_GY + (dev_y + 1) % N_GY]
    came_state = [send_state[:, sources_of[direction], direction] for direction in range(4)]
    came_cell = [send_cell[sources_of[direction], direction] for direction in range(4)]
    droplets_after = jnp.concatenate([own_state] + came_state, 2).reshape(5, -1)
    cells_after = jnp.concatenate([own_cell] + came_cell, 1).reshape(-1)
    return section_rate, droplets_after, cells_after
```

```python
import functools

import jax
import jax.numpy as jnp
from jax import lax
from jax.experimental import pallas as pl
from jax.experimental.pallas import tpu as pltpu
from jax.sharding import PartitionSpec as P

F32 = jnp.float32
BF16 = jnp.bfloat16
I32 = jnp.int32
MESH = pl.DeviceIdType.MESH

STENCIL = (1.6, -0.4, 8.0 / 105.0, -1.0 / 140.0)
SHARES = (0.0, 0.0, 0.0, 0.0, 1.5, -1.0, -2.0, 1.5, 1.5, 0.0, 0.0, 0.0, 0.0, 0.0)
N_F = 14
SLOTS = 8192
ROWS = SLOTS // 128
CAP = 256
TILE = 512


def split(value):
    high = value.astype(BF16)
    low = (value - high.astype(F32)).astype(BF16)
    return high, low


def primitives(q):
    inverse = 1.0 / q[0]
    u = (q[1] * inverse, q[2] * inverse, q[3] * inverse)
    kinetic = 0.5 * (q[1] * q[1] + q[2] * q[2] + q[3] * q[3]) * inverse
    temper = (q[4] - kinetic) * inverse
    return inverse, u, temper, 0.4 * q[0] * temper


def evap_log(temper, q5, inverse):
    return 0.5 * jnp.log(1.0 + temper / (1.0 + q5 * inverse))


def flux(f, axis, value, u, p):
    result = u * value
    if f == axis + 1:
        result = result + p
    if f == 4:
        result = result + p * u
    return result


def gather_kernel(
    n_gx, n_gy,
    fields, fields_y, state, cell_h, new_cell_h, lists_h, counts_h,
    fv, xh, yh, arr, own, own_cell, dep,
    cell, new_cell, lists, counts, st, table, s5, sv, gas, ns, msg,
    in_sem, send_sem, recv_sem,
):
    gx = lax.axis_index("gx")
    gy = lax.axis_index("gy")
    x_next = (lax.rem(gx + 1, n_gx), gy)
    x_prev = (lax.rem(gx + n_gx - 1, n_gx), gy)
    y_next = (gx, lax.rem(gy + 1, n_gy))
    y_prev = (gx, lax.rem(gy + n_gy - 1, n_gy))
    targets = (x_next, x_prev, y_next, y_prev)
    barrier = pltpu.get_barrier_semaphore()
    for device in targets:
        pl.semaphore_signal(barrier, inc=1, device_id=device, device_id_type=MESH)
    loads = [
        pltpu.make_async_copy(src, dst, in_sem.at[i])
        for i, (src, dst) in enumerate(
            (
                (state, st),
                (cell_h, cell),
                (new_cell_h, new_cell),
                (lists_h, lists),
                (counts_h, counts),
                (fields, fv),
            )
        )
    ]
    for copy in loads:
        copy.start()
    pl.semaphore_wait(barrier, 4)
    n_x = fields.shape[1]
    faces = (
        (fields.at[:, n_x - 4 : n_x], xh.at[0]),
        (fields.at[:, 0:4], xh.at[1]),
        (fields_y.at[:, :, 3], yh.at[:, :, 1]),
        (fields_y.at[:, :, 0], yh.at[:, :, 0]),
    )
    sends = [
        pltpu.make_async_remote_copy(
            src_ref=src,
            dst_ref=dst,
            send_sem=send_sem.at[i],
            recv_sem=recv_sem.at[i],
            device_id=targets[i],
            device_id_type=MESH,
        )
        for i, (src, dst) in enumerate(faces)
    ]
    for copy in sends:
        copy.start()
    for copy in loads:
        copy.wait()

    for i in range(ROWS):
        for k in range(5):
            s5[k, i : i + 1, :] = st[k : k + 1, i * 128 : (i + 1) * 128]
    slot = lax.broadcasted_iota(I32, (ROWS, 128), 0) * 128 + lax.broadcasted_iota(
        I32, (ROWS, 128), 1
    )
    live = slot < counts[0:1, 0:1]
    mass = s5[0]
    theta = s5[1]
    size = jnp.exp(jnp.log(mass) * (1.0 / 3.0))
    live_size = jnp.where(live, size, 0.0)
    weights = (
        live_size,
        live_size * s5[2],
        live_size * s5[3],
        live_size * s5[4],
        live_size * theta,
    )
    for k, value in enumerate(weights):
        high, low = split(value)
        sv[k] = high.astype(F32)
        sv[5 + k] = low.astype(F32)

    for h in range(2):
        q = [fv[f, 8 * h : 8 * h + 8].reshape(128, 128) for f in range(6)]
        inverse, u, temper, _ = primitives(q)
        values = (u[0], u[1], u[2], temper, evap_log(temper, q[5], inverse))
        for k, value in enumerate(values):
            high, low = split(value)
            table[k * 128 : (k + 1) * 128, h * 128 : h * 128 + 128] = high
            table[k * 128 : (k + 1) * 128, 256 + h * 128 : 384 + h * 128] = low

    per = TILE // 128
    column_ids = lax.broadcasted_iota(I32, (256, 128), 0)
    row_ids = lax.broadcasted_iota(I32, (128, 128), 0)

    def one_hots(t):
        hots = []
        masks = []
        for j in range(per):
            c = cell[pl.ds(t * per + j, 1), :]
            column = lax.shift_left(lax.shift_right_logical(c, 14), 7) + (c & 127)
            row = lax.shift_right_logical(c, 7) & 127
            hots.append(jnp.where(column_ids == column, 1.0, 0.0).astype(BF16))
            masks.append(row_ids == row)
        return hots, masks

    def gather_step(t, carry):
        hots, masks = one_hots(t)
        for j in range(0, per, 2):
            hot = jnp.concatenate(hots[j : j + 2], 1)
            hot = jnp.concatenate([hot, hot], 0)
            mask = jnp.concatenate(masks[j : j + 2], 1)
            for k in range(5):
                rows = jnp.dot(
                    table[k * 128 : (k + 1) * 128, :], hot, preferred_element_type=F32
                )
                got = jnp.sum(jnp.where(mask, rows, 0.0), axis=0, keepdims=True)
                gas[k, pl.ds(t * per + j, 1), :] = got[:, :128]
                gas[k, pl.ds(t * per + j + 1, 1), :] = got[:, 128:]
        return carry

    lax.fori_loop(0, ROWS // per, gather_step, 0)

    inv_mass = 1.0 / mass
    evap = size * gas[4]
    heat = 0.6 * size * (gas[3] - theta)
    new_state = [
        mass - 0.05 * evap,
        theta + 0.05 * (heat - 0.3 * evap) * inv_mass,
    ]
    for a in range(3):
        v = s5[2 + a]
        new_state.append(v + 0.04 * size * (gas[a] - v) * inv_mass)
    for k in range(5):
        high, low = split(new_state[k])
        ns[k * ROWS : (k + 1) * ROWS, 0:128] = high
        ns[k * ROWS : (k + 1) * ROWS, 128:256] = low
    cells = new_cell[...]
    cell_high = lax.shift_left(lax.shift_right_logical(cells, 8), 8)
    ns[5 * ROWS : 6 * ROWS, 0:128] = cell_high.astype(F32).astype(BF16)
    ns[5 * ROWS : 6 * ROWS, 128:256] = (cells & 255).astype(F32).astype(BF16)

    entry = lax.broadcasted_iota(I32, (1, CAP), 1)
    slot_rows = lax.broadcasted_iota(I32, (ROWS, CAP), 0)
    slot_lanes = lax.broadcasted_iota(I32, (128, CAP), 0)
    departed = jnp.zeros((ROWS, 128), F32)
    for r in range(4):
        picked = lists[r : r + 1, :]
        valid = entry < counts[0:1, 1 + r : 2 + r]
        row_mask = slot_rows == lax.shift_right_logical(picked, 7)
        lane_hot = jnp.where(slot_lanes == (picked & 127), 1.0, 0.0).astype(BF16)
        row_hot = jnp.where(row_mask & valid, 1.0, 0.0).astype(BF16)
        departed += lax.dot_general(
            row_hot, lane_hot, (((1,), (1,)), ((), ())), preferred_element_type=F32
        )
        rows = jnp.dot(
            ns[...], jnp.concatenate([lane_hot, lane_hot], 0), preferred_element_type=F32
        )
        for k in range(6):
            got = jnp.sum(
                jnp.where(row_mask, rows[k * ROWS : (k + 1) * ROWS], 0.0), axis=0, keepdims=True
            )
            msg[r, k : k + 1, :] = jnp.where(valid, got, 0.0 if k < 5 else -1.0)
        msg[r, 6:8, :] = jnp.zeros((2, CAP), F32)
        copy = pltpu.make_async_remote_copy(
            src_ref=msg.at[r],
            dst_ref=arr.at[r],
            send_sem=send_sem.at[4 + r],
            recv_sem=recv_sem.at[4 + r],
            device_id=targets[r],
            device_id_type=MESH,
        )
        copy.start()
        sends.append(copy)
    staying = live & (departed == 0.0)
    own_cell[...] = jnp.where(staying, cells, -1)
    for k in range(5):
        gas[k] = jnp.where(staying, new_state[k], 0.0)
    for i in range(ROWS):
        for k in range(5):
            own[k : k + 1, i * 128 : (i + 1) * 128] = gas[k, i : i + 1, :]

    dep[...] = jnp.zeros_like(dep)

    def deposit_step(t, carry):
        hots, masks = one_hots(t)
        hot = jnp.concatenate(hots + hots, 1)
        for k in range(5):
            parts = [
                jnp.where(masks[j], sv[part + k, pl.ds(t * per + j, 1), :], 0.0).astype(BF16)
                for part in (0, 5)
                for j in range(per)
            ]
            dep[k] += lax.dot_general(
                jnp.concatenate(parts, 1),
                hot,
                (((1,), (1,)), ((), ())),
                preferred_element_type=F32,
            )
        return carry

    lax.fori_loop(0, ROWS // per, deposit_step, 0)
    for copy in sends:
        copy.wait()


def stencil_kernel(
    fv, xh, yh, dep, own, own_cell, arr,
    out, drops, cells,
    uv, pv, wv, ux, px, uy, py, fx, fy,
):
    drops[:, 0:SLOTS] = own[...]
    cells[0:ROWS, :] = own_cell[...]
    for r in range(4):
        drops[:, SLOTS + CAP * r : SLOTS + CAP * (r + 1)] = arr[r, 0:5, :]
        for j in range(2):
            row = ROWS + 2 * r + j
            cells[row : row + 1, :] = arr[r, 5:6, 128 * j : 128 * j + 128].astype(I32)

    def cell_step(x, carry):
        q = [fv[f, x] for f in range(7)]
        inverse, u, temper, p = primitives(q)
        for a in range(3):
            uv[a, x] = u[a]
        pv[x] = p
        wv[x] = 20.0 * q[5] * q[6] * inverse * jnp.exp(-2.0 / temper)
        log = evap_log(temper, q[5], inverse)
        rows = pl.ds(pl.multiple_of(lax.rem(x, 8) * 16, 16), 16)
        lanes = pl.ds(pl.multiple_of(lax.div(x, 8) * 128, 128), 128)
        sums = [dep[k, rows, lanes] for k in range(5)]
        evap = log * sums[0]
        out[0, x] = evap
        out[5, x] = evap
        for a in range(3):
            out[1 + a, x] = (log + 0.8) * sums[1 + a] - 0.8 * u[a] * sums[0]
        out[4, x] = (log + 0.6) * sums[4] - 0.6 * temper * sums[0]
        _, u, _, p = primitives([yh[f, x] for f in range(5)])
        uy[x] = u[1]
        py[x] = p
        return carry

    lax.fori_loop(0, 16, cell_step, 0, unroll=2)
    for s in range(2):
        for i in range(4):
            _, u, _, p = primitives([xh[s, f, i] for f in range(5)])
            ux[s, i] = u[0]
            px[s, i] = p

    for f in range(N_F):
        for s in range(2):
            for i in range(4):
                fx[20 * s + i] = flux(f, 0, xh[s, f, i], ux[s, i], px[s, i])

        def flux_step(x, carry):
            value = fv[f, x]
            fx[4 + x] = flux(f, 0, value, uv[0, x], pv[x])
            edge = flux(f, 1, yh[f, x], uy[x], py[x])
            fy[x, 8:24] = flux(f, 1, value, uv[1, x], pv[x])
            fy[x, 4:8] = edge[4:8]
            fy[x, 24:28] = edge[0:4]
            return carry

        lax.fori_loop(0, 16, flux_step, 0, unroll=8)

        def rate_step(x, carry):
            fz = flux(f, 2, fv[f, x], uv[2, x], pv[x])
            total = None
            for k in range(4):
                term = (
                    (fx[x + 5 + k] - fx[x + 3 - k])
                    + (fy[x, 9 + k : 25 + k] - fy[x, 7 - k : 23 - k])
                    + (pltpu.roll(fz, 127 - k, 1) - pltpu.roll(fz, k + 1, 1))
                )
                total = STENCIL[k] * term if total is None else total + STENCIL[k] * term
            row = -total
            if SHARES[f] != 0.0:
                row = row + SHARES[f] * wv[x]
            if f < 6:
                row = row + out[f, x]
            out[f, x] = row
            return carry

        lax.fori_loop(0, 16, rate_step, 0, unroll=8)


def shape(dims, dtype=F32):
    return jax.ShapeDtypeStruct(dims, dtype)


def per_device(n_gx, n_gy, fields, state, cell, new_cell, lists, counts):
    n_f, n_x, n_y, n_z = fields.shape
    vmem = pl.BlockSpec(memory_space=pltpu.VMEM)
    hbm = pl.BlockSpec(memory_space=pltpu.HBM)
    fv, xh, yh, arr, own, own_cell, dep = pl.pallas_call(
        functools.partial(gather_kernel, n_gx, n_gy),
        out_shape=(
            shape((n_f, n_x, n_y, n_z)),
            shape((2, n_f, 4, n_y, n_z)),
            shape((n_f, n_x, 2, 4, n_z)),
            shape((4, 8, CAP)),
            shape((5, SLOTS)),
            shape((ROWS, 128), I32),
            shape((5, 128, 256)),
        ),
        in_specs=[hbm] * 7,
        out_specs=(vmem,) * 7,
        scratch_shapes=[
            pltpu.VMEM((ROWS, 128), I32),
            pltpu.VMEM((ROWS, 128), I32),
            pltpu.VMEM((4, CAP), I32),
            pltpu.VMEM((1, 5), I32),
            pltpu.VMEM((5, SLOTS), F32),
            pltpu.VMEM((640, 512), BF16),
            pltpu.VMEM((5, ROWS, 128), F32),
            pltpu.VMEM((10, ROWS, 128), F32),
            pltpu.VMEM((5, ROWS, 128), F32),
            pltpu.VMEM((6 * ROWS, 256), BF16),
            pltpu.VMEM((4, 8, CAP), F32),
            pltpu.SemaphoreType.DMA((6,)),
            pltpu.SemaphoreType.DMA((8,)),
            pltpu.SemaphoreType.DMA((8,)),
        ],
        compiler_params=pltpu.CompilerParams(
            collective_id=0, has_side_effects=True, vmem_limit_bytes=24 << 20
        ),
        name="droplets",
    )(
        *(
            pltpu.with_memory_space_constraint(a, pltpu.HBM)
            for a in (
                fields,
                fields.reshape(n_f, n_x, n_y // 4, 4, n_z),
                state,
                cell.reshape(ROWS, 128),
                new_cell.reshape(ROWS, 128),
                lists,
                counts,
            )
        )
    )
    out, drops, cells = pl.pallas_call(
        stencil_kernel,
        grid=(1,),
        out_shape=(
            shape((n_f, n_x, n_y, n_z)),
            shape((5, SLOTS + 4 * CAP)),
            shape((ROWS + 8, 128), I32),
        ),
        in_specs=[vmem] * 7,
        out_specs=tuple(
            pl.BlockSpec(s, lambda i, n=len(s): (0,) * n)
            for s in ((n_f, n_x, n_y, n_z), (5, SLOTS + 4 * CAP), (ROWS + 8, 128))
        ),
        scratch_shapes=[
            pltpu.VMEM((3, 16, 16, 128), F32),
            pltpu.VMEM((16, 16, 128), F32),
            pltpu.VMEM((16, 16, 128), F32),
            pltpu.VMEM((2, 4, 16, 128), F32),
            pltpu.VMEM((2, 4, 16, 128), F32),
            pltpu.VMEM((16, 8, 128), F32),
            pltpu.VMEM((16, 8, 128), F32),
            pltpu.VMEM((24, 16, 128), F32),
            pltpu.VMEM((16, 32, 128), F32),
        ],
        compiler_params=pltpu.CompilerParams(vmem_limit_bytes=24 << 20),
        name="stencil",
    )(fv, xh, yh.reshape(n_f, n_x, 8, n_z), dep, own, own_cell, arr)
    return out, drops, cells.reshape(-1)


def solution(mesh):
    placed = (
        P(None, "gx", "gy", None),
        P(None, ("gx", "gy")),
        P(("gx", "gy")),
        P(("gx", "gy")),
        P(("gx", "gy"), None),
        P(("gx", "gy"), None),
    )
    return jax.shard_map(
        functools.partial(per_device, mesh.shape["gx"], mesh.shape["gy"]),
        mesh=mesh,
        in_specs=placed,
        out_specs=(P(None, "gx", "gy", None), P(None, ("gx", "gy")), P(("gx", "gy"))),
        check_vma=False,
    )
```

```python
import functools

import jax
import jax.numpy as jnp
from jax import lax
from jax.experimental import pallas as pl
from jax.experimental.pallas import tpu as pltpu
from jax.sharding import PartitionSpec as P

F32 = jnp.float32
BF16 = jnp.bfloat16
I32 = jnp.int32
MESH = pl.DeviceIdType.MESH

STENCIL = (1.6, -0.4, 8.0 / 105.0, -1.0 / 140.0)
SHARES = (0.0, 0.0, 0.0, 0.0, 1.5, -1.0, -2.0, 1.5, 1.5, 0.0, 0.0, 0.0, 0.0, 0.0)
N_F = 14
SLOTS = 8192
ROWS = SLOTS // 128
CAP = 256
TILE = 1024


def split(value):
    high = value.astype(BF16)
    low = (value - high.astype(F32)).astype(BF16)
    return high, low


def primitives(q):
    inverse = 1.0 / q[0]
    u = (q[1] * inverse, q[2] * inverse, q[3] * inverse)
    kinetic = 0.5 * (q[1] * q[1] + q[2] * q[2] + q[3] * q[3]) * inverse
    temper = (q[4] - kinetic) * inverse
    return inverse, u, temper, 0.4 * q[0] * temper


def evap_log(temper, q5, inverse):
    return 0.5 * jnp.log(1.0 + temper / (1.0 + q5 * inverse))


def flux(f, axis, value, u, p):
    result = u * value
    if f == axis + 1:
        result = result + p
    if f == 4:
        result = result + p * u
    return result


def droplet_kernel(
    n_gx, n_gy,
    fields, fields_y, state, cell_h, new_cell_h, lists_h, counts_h,
    part, xh, yh, arr, own, own_cell,
    fv, cell, new_cell, lists, counts, st, table, s5, sv, gas, ns, msg, dep,
    uv, pv, wv, fx, fy,
    in_sem, send_sem, recv_sem,
):
    gx = lax.axis_index("gx")
    gy = lax.axis_index("gy")
    x_next = (lax.rem(gx + 1, n_gx), gy)
    x_prev = (lax.rem(gx + n_gx - 1, n_gx), gy)
    y_next = (gx, lax.rem(gy + 1, n_gy))
    y_prev = (gx, lax.rem(gy + n_gy - 1, n_gy))
    targets = (x_next, x_prev, y_next, y_prev)
    barrier = pltpu.get_barrier_semaphore()
    for device in targets:
        pl.semaphore_signal(barrier, inc=1, device_id=device, device_id_type=MESH)
    loads = [
        pltpu.make_async_copy(src, dst, in_sem.at[i])
        for i, (src, dst) in enumerate(
            (
                (state, st),
                (cell_h, cell),
                (new_cell_h, new_cell),
                (lists_h, lists),
                (counts_h, counts),
                (fields, fv),
            )
        )
    ]
    for copy in loads:
        copy.start()
    pl.semaphore_wait(barrier, 4)
    n_x = fields.shape[1]
    faces = (
        (fields.at[:, n_x - 4 : n_x], xh.at[0]),
        (fields.at[:, 0:4], xh.at[1]),
        (fields_y.at[:, :, 3], yh.at[:, :, 1]),
        (fields_y.at[:, :, 0], yh.at[:, :, 0]),
    )
    sends = [
        pltpu.make_async_remote_copy(
            src_ref=src,
            dst_ref=dst,
            send_sem=send_sem.at[i],
            recv_sem=recv_sem.at[i],
            device_id=targets[i],
            device_id_type=MESH,
        )
        for i, (src, dst) in enumerate(faces)
    ]
    for copy in sends:
        copy.start()
    for copy in loads:
        copy.wait()

    for i in range(ROWS):
        for k in range(5):
            s5[k, i : i + 1, :] = st[k : k + 1, i * 128 : (i + 1) * 128]
    slot = lax.broadcasted_iota(I32, (ROWS, 128), 0) * 128 + lax.broadcasted_iota(
        I32, (ROWS, 128), 1
    )
    live = slot < counts[0:1, 0:1]
    mass = s5[0]
    theta = s5[1]
    size = jnp.exp(jnp.log(mass) * (1.0 / 3.0))
    live_size = jnp.where(live, size, 0.0)
    weights = (
        live_size,
        live_size * s5[2],
        live_size * s5[3],
        live_size * s5[4],
        live_size * theta,
    )
    for k, value in enumerate(weights):
        high, low = split(value)
        sv[k] = high.astype(F32)
        sv[5 + k] = low.astype(F32)

    for h in range(2):
        q = [fv[f, 8 * h : 8 * h + 8].reshape(128, 128) for f in range(6)]
        inverse, u, temper, _ = primitives(q)
        values = (u[0], u[1], u[2], temper, evap_log(temper, q[5], inverse))
        for k, value in enumerate(values):
            high, low = split(value)
            table[k * 128 : (k + 1) * 128, h * 128 : h * 128 + 128] = high
            table[k * 128 : (k + 1) * 128, 256 + h * 128 : 384 + h * 128] = low

    per = TILE // 128
    column_ids = lax.broadcasted_iota(I32, (256, 128), 0)
    row_ids = lax.broadcasted_iota(I32, (128, 128), 0)
    dep[...] = jnp.zeros_like(dep)

    def droplet_step(t, carry):
        hots = []
        masks = []
        for j in range(per):
            c = cell[pl.ds(t * per + j, 1), :]
            column = lax.shift_left(lax.shift_right_logical(c, 14), 7) + (c & 127)
            row = lax.shift_right_logical(c, 7) & 127
            hots.append(jnp.where(column_ids == column, 1.0, 0.0).astype(BF16))
            masks.append(row_ids == row)
        for j in range(0, per, 2):
            hot = jnp.concatenate(hots[j : j + 2], 1)
            rows = jnp.dot(
                table[...], jnp.concatenate([hot, hot], 0), preferred_element_type=F32
            )
            mask = jnp.concatenate(masks[j : j + 2], 1)
            for k in range(5):
                got = jnp.sum(
                    jnp.where(mask, rows[k * 128 : (k + 1) * 128], 0.0), axis=0, keepdims=True
                )
                gas[k, pl.ds(t * per + j, 1), :] = got[:, :128]
                gas[k, pl.ds(t * per + j + 1, 1), :] = got[:, 128:]
        lefts = []
        for k in range(5):
            parts = [
                jnp.where(masks[j], sv[half + k, pl.ds(t * per + j, 1), :], 0.0).astype(BF16)
                for half in (0, 5)
                for j in range(per)
            ]
            lefts.append(jnp.concatenate(parts, 1))
        sums = lax.dot_general(
            jnp.concatenate(lefts, 0),
            jnp.concatenate(hots + hots, 1),
            (((1,), (1,)), ((), ())),
            preferred_element_type=F32,
        )
        for k in range(5):
            dep[k] += sums[k * 128 : (k + 1) * 128]
        return carry

    lax.fori_loop(0, ROWS // per, droplet_step, 0)

    inv_mass = 1.0 / mass
    evap = size * gas[4]
    heat = 0.6 * size * (gas[3] - theta)
    new_state = [
        mass - 0.05 * evap,
        theta + 0.05 * (heat - 0.3 * evap) * inv_mass,
    ]
    for a in range(3):
        v = s5[2 + a]
        new_state.append(v + 0.04 * size * (gas[a] - v) * inv_mass)
    for k in range(5):
        high, low = split(new_state[k])
        ns[k * ROWS : (k + 1) * ROWS, 0:128] = high
        ns[k * ROWS : (k + 1) * ROWS, 128:256] = low
    cells = new_cell[...]
    cell_high = lax.shift_left(lax.shift_right_logical(cells, 8), 8)
    ns[5 * ROWS : 6 * ROWS, 0:128] = cell_high.astype(F32).astype(BF16)
    ns[5 * ROWS : 6 * ROWS, 128:256] = (cells & 255).astype(F32).astype(BF16)

    entry = lax.broadcasted_iota(I32, (1, CAP), 1)
    slot_rows = lax.broadcasted_iota(I32, (ROWS, CAP), 0)
    slot_lanes = lax.broadcasted_iota(I32, (128, CAP), 0)
    departed = jnp.zeros((ROWS, 128), F32)
    for r in range(4):
        picked = lists[r : r + 1, :]
        valid = entry < counts[0:1, 1 + r : 2 + r]
        row_mask = slot_rows == lax.shift_right_logical(picked, 7)
        lane_hot = jnp.where(slot_lanes == (picked & 127), 1.0, 0.0).astype(BF16)
        row_hot = jnp.where(row_mask & valid, 1.0, 0.0).astype(BF16)
        departed += lax.dot_general(
            row_hot, lane_hot, (((1,), (1,)), ((), ())), preferred_element_type=F32
        )
        rows = jnp.dot(
            ns[...], jnp.concatenate([lane_hot, lane_hot], 0), preferred_element_type=F32
        )
        for k in range(6):
            got = jnp.sum(
                jnp.where(row_mask, rows[k * ROWS : (k + 1) * ROWS], 0.0), axis=0, keepdims=True
            )
            msg[r, k : k + 1, :] = jnp.where(valid, got, 0.0 if k < 5 else -1.0)
        msg[r, 6:8, :] = jnp.zeros((2, CAP), F32)
        copy = pltpu.make_async_remote_copy(
            src_ref=msg.at[r],
            dst_ref=arr.at[r],
            send_sem=send_sem.at[4 + r],
            recv_sem=recv_sem.at[4 + r],
            device_id=targets[r],
            device_id_type=MESH,
        )
        copy.start()
        sends.append(copy)
    staying = live & (departed == 0.0)
    own_cell[...] = jnp.where(staying, cells, -1)
    for k in range(5):
        gas[k] = jnp.where(staying, new_state[k], 0.0)
    for i in range(ROWS):
        for k in range(5):
            own[k : k + 1, i * 128 : (i + 1) * 128] = gas[k, i : i + 1, :]

    def cell_step(x, carry):
        q = [fv[f, x] for f in range(7)]
        inverse, u, temper, p = primitives(q)
        for a in range(3):
            uv[a, x] = u[a]
        pv[x] = p
        wv[x] = 20.0 * q[5] * q[6] * inverse * jnp.exp(-2.0 / temper)
        log = evap_log(temper, q[5], inverse)
        rows = pl.ds(pl.multiple_of(lax.rem(x, 8) * 16, 16), 16)
        lanes = pl.ds(pl.multiple_of(lax.div(x, 8) * 128, 128), 128)
        sums = [dep[k, rows, lanes] for k in range(5)]
        evap = log * sums[0]
        part[0, x] = evap
        part[5, x] = evap
        for a in range(3):
            part[1 + a, x] = (log + 0.8) * sums[1 + a] - 0.8 * u[a] * sums[0]
        part[4, x] = (log + 0.6) * sums[4] - 0.6 * temper * sums[0]
        return carry

    lax.fori_loop(0, 16, cell_step, 0, unroll=2)
    blank = jnp.zeros((4, 16, 128), F32)
    fx[0:4] = blank
    fx[20:24] = blank
    for x in range(16):
        fy[x, 0:8] = jnp.zeros((8, 128), F32)
        fy[x, 24:32] = jnp.zeros((8, 128), F32)
    for f in range(N_F):

        def flux_step(x, carry):
            value = fv[f, x]
            fx[4 + x] = flux(f, 0, value, uv[0, x], pv[x])
            fy[x, 8:24] = flux(f, 1, value, uv[1, x], pv[x])
            return carry

        lax.fori_loop(0, 16, flux_step, 0, unroll=8)

        def rate_step(x, carry):
            fz = flux(f, 2, fv[f, x], uv[2, x], pv[x])
            total = None
            for k in range(4):
                term = (
                    (fx[x + 5 + k] - fx[x + 3 - k])
                    + (fy[x, 9 + k : 25 + k] - fy[x, 7 - k : 23 - k])
                    + (pltpu.roll(fz, 127 - k, 1) - pltpu.roll(fz, k + 1, 1))
                )
                total = STENCIL[k] * term if total is None else total + STENCIL[k] * term
            row = -total
            if SHARES[f] != 0.0:
                row = row + SHARES[f] * wv[x]
            if f < 6:
                row = row + part[f, x]
            part[f, x] = row
            return carry

        lax.fori_loop(0, 16, rate_step, 0, unroll=8)
    for copy in sends:
        copy.wait()


def edge_kernel(
    part, xh, yh, own, own_cell, arr,
    out_h, drops_h, cells_h,
    out, drops, cells, ux, px, uy, py, sem,
):
    drops[:, 0:SLOTS] = own[...]
    cells[0:ROWS, :] = own_cell[...]
    for r in range(4):
        drops[:, SLOTS + CAP * r : SLOTS + CAP * (r + 1)] = arr[r, 0:5, :]
        for j in range(2):
            row = ROWS + 2 * r + j
            cells[row : row + 1, :] = arr[r, 5:6, 128 * j : 128 * j + 128].astype(I32)
    copies = [
        pltpu.make_async_copy(drops, drops_h, sem.at[N_F]),
        pltpu.make_async_copy(cells, cells_h, sem.at[N_F + 1]),
    ]
    for copy in copies:
        copy.start()

    def cell_step(x, carry):
        _, u, _, p = primitives([yh[f, x] for f in range(5)])
        uy[x] = u[1]
        py[x] = p
        return carry

    lax.fori_loop(0, 16, cell_step, 0, unroll=4)
    for s in range(2):
        for i in range(4):
            _, u, _, p = primitives([xh[s, f, i] for f in range(5)])
            ux[s, i] = u[0]
            px[s, i] = p

    row = lax.broadcasted_iota(I32, (8, 128), 0)
    zero = jnp.zeros((8, 128), F32)
    down = [jnp.where(row < k + 1, -STENCIL[k], 0.0) for k in range(4)]
    up = [jnp.where(row >= 7 - k, STENCIL[k], 0.0) for k in range(4)]
    for f in range(N_F):

        def y_step(x, carry):
            edge = flux(f, 1, yh[f, x], uy[x], py[x])
            total = (down[3] + up[3]) * pltpu.roll(edge, 4, 0)
            for k in range(3):
                total = total + down[k] * pltpu.roll(edge, k + 1, 0)
                total = total + up[k] * pltpu.roll(edge, 7 - k, 0)
            out[f, x, 0:8] = part[f, x, 0:8] - jnp.where(row < 4, total, zero)
            out[f, x, 8:16] = part[f, x, 8:16] - jnp.where(row < 4, zero, total)
            return carry

        lax.fori_loop(0, 16, y_step, 0, unroll=8)
        low = [flux(f, 0, xh[0, f, i], ux[0, i], px[0, i]) for i in range(4)]
        high = [flux(f, 0, xh[1, f, i], ux[1, i], px[1, i]) for i in range(4)]
        for x in range(4):
            total = None
            for k in range(x, 4):
                term = STENCIL[k] * low[3 + x - k]
                total = term if total is None else total + term
            out[f, x] += total
            total = None
            for k in range(x, 4):
                term = STENCIL[k] * high[k - x]
                total = term if total is None else total + term
            out[f, 15 - x] -= total
        copy = pltpu.make_async_copy(out.at[f], out_h.at[f], sem.at[f])
        copy.start()
        copies.append(copy)
    for copy in copies:
        copy.wait()


def shape(dims, dtype=F32):
    return jax.ShapeDtypeStruct(dims, dtype)


def per_device(n_gx, n_gy, fields, state, cell, new_cell, lists, counts):
    n_f, n_x, n_y, n_z = fields.shape
    vmem = pl.BlockSpec(memory_space=pltpu.VMEM)
    hbm = pl.BlockSpec(memory_space=pltpu.HBM)
    cube = (n_x, n_y, n_z)
    part, xh, yh, arr, own, own_cell = pl.pallas_call(
        functools.partial(droplet_kernel, n_gx, n_gy),
        out_shape=(
            shape((n_f,) + cube),
            shape((2, n_f, 4, n_y, n_z)),
            shape((n_f, n_x, 2, 4, n_z)),
            shape((4, 8, CAP)),
            shape((5, SLOTS)),
            shape((ROWS, 128), I32),
        ),
        in_specs=[hbm] * 7,
        out_specs=(vmem,) * 6,
        scratch_shapes=[
            pltpu.VMEM((n_f,) + cube, F32),
            pltpu.VMEM((ROWS, 128), I32),
            pltpu.VMEM((ROWS, 128), I32),
            pltpu.VMEM((4, CAP), I32),
            pltpu.VMEM((1, 5), I32),
            pltpu.VMEM((5, SLOTS), F32),
            pltpu.VMEM((640, 512), BF16),
            pltpu.VMEM((5, ROWS, 128), F32),
            pltpu.VMEM((10, ROWS, 128), F32),
            pltpu.VMEM((5, ROWS, 128), F32),
            pltpu.VMEM((6 * ROWS, 256), BF16),
            pltpu.VMEM((4, 8, CAP), F32),
            pltpu.VMEM((5, 128, 256), F32),
            pltpu.VMEM((3,) + cube, F32),
            pltpu.VMEM(cube, F32),
            pltpu.VMEM(cube, F32),
            pltpu.VMEM((n_x + 8, n_y, n_z), F32),
            pltpu.VMEM((n_x, n_y + 16, n_z), F32),
            pltpu.SemaphoreType.DMA((6,)),
            pltpu.SemaphoreType.DMA((8,)),
            pltpu.SemaphoreType.DMA((8,)),
        ],
        compiler_params=pltpu.CompilerParams(
            collective_id=0, has_side_effects=True, vmem_limit_bytes=36 << 20
        ),
        name="droplets",
    )(
        *(
            pltpu.with_memory_space_constraint(a, pltpu.HBM)
            for a in (
                fields,
                fields.reshape(n_f, n_x, n_y // 4, 4, n_z),
                state,
                cell.reshape(ROWS, 128),
                new_cell.reshape(ROWS, 128),
                lists,
                counts,
            )
        )
    )
    out, drops, cells = pl.pallas_call(
        edge_kernel,
        out_shape=(
            shape((n_f,) + cube),
            shape((5, SLOTS + 4 * CAP)),
            shape((ROWS + 8, 128), I32),
        ),
        in_specs=[vmem] * 6,
        out_specs=(hbm,) * 3,
        scratch_shapes=[
            pltpu.VMEM((n_f,) + cube, F32),
            pltpu.VMEM((5, SLOTS + 4 * CAP), F32),
            pltpu.VMEM((ROWS + 8, 128), I32),
            pltpu.VMEM((2, 4, n_y, n_z), F32),
            pltpu.VMEM((2, 4, n_y, n_z), F32),
            pltpu.VMEM((n_x, 8, n_z), F32),
            pltpu.VMEM((n_x, 8, n_z), F32),
            pltpu.SemaphoreType.DMA((n_f + 2,)),
        ],
        compiler_params=pltpu.CompilerParams(vmem_limit_bytes=24 << 20),
        name="edges",
    )(part, xh, yh.reshape(n_f, n_x, 8, n_z), own, own_cell, arr)
    return out, drops, cells.reshape(-1)


def solution(mesh):
    placed = (
        P(None, "gx", "gy", None),
        P(None, ("gx", "gy")),
        P(("gx", "gy")),
        P(("gx", "gy")),
        P(("gx", "gy"), None),
        P(("gx", "gy"), None),
    )
    return jax.shard_map(
        functools.partial(per_device, mesh.shape["gx"], mesh.shape["gy"]),
        mesh=mesh,
        in_specs=placed,
        out_specs=(P(None, "gx", "gy", None), P(None, ("gx", "gy")), P(("gx", "gy"))),
        check_vma=False,
    )
```

```python
import functools

import jax
import jax.numpy as jnp
from jax import lax
from jax.experimental import pallas as pl
from jax.experimental.pallas import tpu as pltpu
from jax.sharding import PartitionSpec as P

F32 = jnp.float32
BF16 = jnp.bfloat16
I32 = jnp.int32
MESH = pl.DeviceIdType.MESH

STENCIL = (1.6, -0.4, 8.0 / 105.0, -1.0 / 140.0)
SHARES = (0.0, 0.0, 0.0, 0.0, 1.5, -1.0, -2.0, 1.5, 1.5, 0.0, 0.0, 0.0, 0.0, 0.0)
N_F = 14
SLOTS = 8192
ROWS = SLOTS // 128
CAP = 256
TILE = 2048


def split(value):
    high = value.astype(BF16)
    low = (value - high.astype(F32)).astype(BF16)
    return high, low


def primitives(q):
    inverse = 1.0 / q[0]
    u = (q[1] * inverse, q[2] * inverse, q[3] * inverse)
    kinetic = 0.5 * (q[1] * q[1] + q[2] * q[2] + q[3] * q[3]) * inverse
    temper = (q[4] - kinetic) * inverse
    return inverse, u, temper, 0.4 * q[0] * temper


def evap_log(temper, q5, inverse):
    return 0.5 * jnp.log(1.0 + temper / (1.0 + q5 * inverse))


def flux(f, axis, value, u, p):
    result = u * value
    if f == axis + 1:
        result = result + p
    if f == 4:
        result = result + p * u
    return result


def droplet_kernel(
    n_gx, n_gy,
    fields, fields_y, state, cell_h, new_cell_h, lists_h, counts_h,
    part, xh, yh, arr, own, own_cell,
    fv, cell, new_cell, lists, counts, st, table, s5, sv, gas, ns, msg, dep,
    uv, pv, wv, tv, lv, fx, fy,
    in_sem, send_sem, recv_sem,
):
    gx = lax.axis_index("gx")
    gy = lax.axis_index("gy")
    x_next = (lax.rem(gx + 1, n_gx), gy)
    x_prev = (lax.rem(gx + n_gx - 1, n_gx), gy)
    y_next = (gx, lax.rem(gy + 1, n_gy))
    y_prev = (gx, lax.rem(gy + n_gy - 1, n_gy))
    targets = (x_next, x_prev, y_next, y_prev)
    barrier = pltpu.get_barrier_semaphore()
    for device in targets:
        pl.semaphore_signal(barrier, inc=1, device_id=device, device_id_type=MESH)
    loads = [
        pltpu.make_async_copy(src, dst, in_sem.at[i])
        for i, (src, dst) in enumerate(
            (
                (state, st),
                (cell_h, cell),
                (new_cell_h, new_cell),
                (lists_h, lists),
                (counts_h, counts),
                (fields, fv),
            )
        )
    ]
    for copy in loads:
        copy.start()
    pl.semaphore_wait(barrier, 4)
    n_x = fields.shape[1]
    faces = (
        (fields.at[:, n_x - 4 : n_x], xh.at[0]),
        (fields.at[:, 0:4], xh.at[1]),
        (fields_y.at[:, :, 3], yh.at[:, :, 1]),
        (fields_y.at[:, :, 0], yh.at[:, :, 0]),
    )
    sends = [
        pltpu.make_async_remote_copy(
            src_ref=src,
            dst_ref=dst,
            send_sem=send_sem.at[i],
            recv_sem=recv_sem.at[i],
            device_id=targets[i],
            device_id_type=MESH,
        )
        for i, (src, dst) in enumerate(faces)
    ]
    for i in (2, 0, 3, 1):
        sends[i].start()
    for copy in loads:
        copy.wait()

    for i in range(ROWS):
        for k in range(5):
            s5[k, i : i + 1, :] = st[k : k + 1, i * 128 : (i + 1) * 128]
    slot = lax.broadcasted_iota(I32, (ROWS, 128), 0) * 128 + lax.broadcasted_iota(
        I32, (ROWS, 128), 1
    )
    live = slot < counts[0:1, 0:1]
    mass = s5[0]
    theta = s5[1]
    size = jnp.exp(jnp.log(mass) * (1.0 / 3.0))
    live_size = jnp.where(live, size, 0.0)
    weights = (
        live_size,
        live_size * s5[2],
        live_size * s5[3],
        live_size * s5[4],
        live_size * theta,
    )
    for k, value in enumerate(weights):
        high, low = split(value)
        sv[k] = high.astype(F32)
        sv[5 + k] = low.astype(F32)

    def cell_step(x, carry):
        q = [fv[f, x] for f in range(7)]
        inverse, u, temper, p = primitives(q)
        for a in range(3):
            uv[a, x] = u[a]
        pv[x] = p
        tv[x] = temper
        lv[x] = evap_log(temper, q[5], inverse)
        wv[x] = 20.0 * q[5] * q[6] * inverse * jnp.exp(-2.0 / temper)
        return carry

    lax.fori_loop(0, 16, cell_step, 0, unroll=2)

    for h in range(2):
        values = [v[8 * h : 8 * h + 8].reshape(128, 128) for v in (uv.at[0], uv.at[1], uv.at[2], tv, lv)]
        for k, value in enumerate(values):
            high, low = split(value)
            table[k * 128 : (k + 1) * 128, h * 128 : h * 128 + 128] = high
            table[k * 128 : (k + 1) * 128, 256 + h * 128 : 384 + h * 128] = low

    per = TILE // 128
    planes = 16 * per // ROWS
    column_ids = lax.broadcasted_iota(I32, (256, 128), 0)
    row_ids = lax.broadcasted_iota(I32, (128, 128), 0)
    dep[...] = jnp.zeros_like(dep)

    def droplet_step(t, carry):
        hots = []
        masks = []
        for j in range(per):
            c = cell[pl.ds(t * per + j, 1), :]
            column = lax.shift_left(lax.shift_right_logical(c, 14), 7) + (c & 127)
            row = lax.shift_right_logical(c, 7) & 127
            hots.append(jnp.where(column_ids == column, 1.0, 0.0).astype(BF16))
            masks.append(row_ids == row)
        for j in range(0, per, 2):
            hot = jnp.concatenate(hots[j : j + 2], 1)
            rows = jnp.dot(
                table[...], jnp.concatenate([hot, hot], 0), preferred_element_type=F32
            )
            mask = jnp.concatenate(masks[j : j + 2], 1)
            for k in range(5):
                got = jnp.sum(
                    jnp.where(mask, rows[k * 128 : (k + 1) * 128], 0.0), axis=0, keepdims=True
                )
                gas[k, pl.ds(t * per + j, 1), :] = got[:, :128]
                gas[k, pl.ds(t * per + j + 1, 1), :] = got[:, 128:]
        lefts = []
        for k in range(5):
            parts = [
                jnp.where(masks[j], sv[half + k, pl.ds(t * per + j, 1), :], 0.0).astype(BF16)
                for half in (0, 5)
                for j in range(per)
            ]
            lefts.append(jnp.concatenate(parts, 1))
        sums = lax.dot_general(
            jnp.concatenate(lefts, 0),
            jnp.concatenate(hots + hots, 1),
            (((1,), (1,)), ((), ())),
            preferred_element_type=F32,
        )
        for k in range(5):
            dep[k] += sums[k * 128 : (k + 1) * 128]
        for i in range(planes):
            x = t * planes + i
            uz = uv[2, x]
            p = pv[x]
            for f in range(N_F):
                fz = flux(f, 2, fv[f, x], uz, p)
                total = None
                for k in range(4):
                    term = STENCIL[k] * (pltpu.roll(fz, 127 - k, 1) - pltpu.roll(fz, k + 1, 1))
                    total = term if total is None else total + term
                if SHARES[f] != 0.0:
                    part[f, x] = SHARES[f] * wv[x] - total
                else:
                    part[f, x] = -total
        return carry

    lax.fori_loop(0, ROWS // per, droplet_step, 0)

    inv_mass = 1.0 / mass
    evap = size * gas[4]
    heat = 0.6 * size * (gas[3] - theta)
    new_state = [
        mass - 0.05 * evap,
        theta + 0.05 * (heat - 0.3 * evap) * inv_mass,
    ]
    for a in range(3):
        v = s5[2 + a]
        new_state.append(v + 0.04 * size * (gas[a] - v) * inv_mass)
    for k in range(5):
        high, low = split(new_state[k])
        ns[k * ROWS : (k + 1) * ROWS, 0:128] = high
        ns[k * ROWS : (k + 1) * ROWS, 128:256] = low
    cells = new_cell[...]
    cell_high = lax.shift_left(lax.shift_right_logical(cells, 8), 8)
    ns[5 * ROWS : 6 * ROWS, 0:128] = cell_high.astype(F32).astype(BF16)
    ns[5 * ROWS : 6 * ROWS, 128:256] = (cells & 255).astype(F32).astype(BF16)

    entry = lax.broadcasted_iota(I32, (1, CAP), 1)
    slot_rows = lax.broadcasted_iota(I32, (ROWS, CAP), 0)
    slot_lanes = lax.broadcasted_iota(I32, (128, CAP), 0)
    departed = jnp.zeros((ROWS, 128), F32)
    for r in range(4):
        picked = lists[r : r + 1, :]
        valid = entry < counts[0:1, 1 + r : 2 + r]
        row_mask = slot_rows == lax.shift_right_logical(picked, 7)
        lane_hot = jnp.where(slot_lanes == (picked & 127), 1.0, 0.0).astype(BF16)
        row_hot = jnp.where(row_mask & valid, 1.0, 0.0).astype(BF16)
        departed += lax.dot_general(
            row_hot, lane_hot, (((1,), (1,)), ((), ())), preferred_element_type=F32
        )
        rows = jnp.dot(
            ns[...], jnp.concatenate([lane_hot, lane_hot], 0), preferred_element_type=F32
        )
        for k in range(6):
            got = jnp.sum(
                jnp.where(row_mask, rows[k * ROWS : (k + 1) * ROWS], 0.0), axis=0, keepdims=True
            )
            msg[r, k : k + 1, :] = jnp.where(valid, got, 0.0 if k < 5 else -1.0)
        msg[r, 6:8, :] = jnp.zeros((2, CAP), F32)
        copy = pltpu.make_async_remote_copy(
            src_ref=msg.at[r],
            dst_ref=arr.at[r],
            send_sem=send_sem.at[4 + r],
            recv_sem=recv_sem.at[4 + r],
            device_id=targets[r],
            device_id_type=MESH,
        )
        copy.start()
        sends.append(copy)
    staying = live & (departed == 0.0)
    own_cell[...] = jnp.where(staying, cells, -1)
    for k in range(5):
        gas[k] = jnp.where(staying, new_state[k], 0.0)
    for i in range(ROWS):
        for k in range(5):
            own[k : k + 1, i * 128 : (i + 1) * 128] = gas[k, i : i + 1, :]

    def deposit_step(x, carry):
        u = [uv[a, x] for a in range(3)]
        log = lv[x]
        rows = pl.ds(pl.multiple_of(lax.rem(x, 8) * 16, 16), 16)
        lanes = pl.ds(pl.multiple_of(lax.div(x, 8) * 128, 128), 128)
        sums = [dep[k, rows, lanes] for k in range(5)]
        evap = log * sums[0]
        part[0, x] += evap
        part[5, x] += evap
        for a in range(3):
            part[1 + a, x] += (log + 0.8) * sums[1 + a] - 0.8 * u[a] * sums[0]
        part[4, x] += (log + 0.6) * sums[4] - 0.6 * tv[x] * sums[0]
        return carry

    lax.fori_loop(0, 16, deposit_step, 0, unroll=2)
    blank = jnp.zeros((4, 16, 128), F32)
    fx[0:4] = blank
    fx[20:24] = blank
    for x in range(16):
        fy[x, 0:8] = jnp.zeros((8, 128), F32)
        fy[x, 24:32] = jnp.zeros((8, 128), F32)
    for f in range(N_F):

        def flux_step(x, carry):
            value = fv[f, x]
            fx[4 + x] = flux(f, 0, value, uv[0, x], pv[x])
            fy[x, 8:24] = flux(f, 1, value, uv[1, x], pv[x])
            return carry

        lax.fori_loop(0, 16, flux_step, 0, unroll=8)

        def rate_step(x, carry):
            total = None
            for k in range(4):
                term = (fx[x + 5 + k] - fx[x + 3 - k]) + (
                    fy[x, 9 + k : 25 + k] - fy[x, 7 - k : 23 - k]
                )
                total = STENCIL[k] * term if total is None else total + STENCIL[k] * term
            part[f, x] -= total
            return carry

        lax.fori_loop(0, 16, rate_step, 0, unroll=8)
    for copy in sends:
        copy.wait()


def edge_kernel(
    part, xh, yh, own, own_cell, arr,
    out_h, drops_h, cells_h,
    out, drops, cells, ux, px, uy, py, sem,
):
    drops[:, 0:SLOTS] = own[...]
    cells[0:ROWS, :] = own_cell[...]
    for r in range(4):
        drops[:, SLOTS + CAP * r : SLOTS + CAP * (r + 1)] = arr[r, 0:5, :]
        for j in range(2):
            row = ROWS + 2 * r + j
            cells[row : row + 1, :] = arr[r, 5:6, 128 * j : 128 * j + 128].astype(I32)
    copies = [
        pltpu.make_async_copy(drops, drops_h, sem.at[N_F]),
        pltpu.make_async_copy(cells, cells_h, sem.at[N_F + 1]),
    ]
    for copy in copies:
        copy.start()

    def cell_step(x, carry):
        _, u, _, p = primitives([yh[f, x] for f in range(5)])
        uy[x] = u[1]
        py[x] = p
        return carry

    lax.fori_loop(0, 16, cell_step, 0, unroll=4)
    for s in range(2):
        for i in range(4):
            _, u, _, p = primitives([xh[s, f, i] for f in range(5)])
            ux[s, i] = u[0]
            px[s, i] = p

    row = lax.broadcasted_iota(I32, (8, 128), 0)
    zero = jnp.zeros((8, 128), F32)
    down = [jnp.where(row < k + 1, -STENCIL[k], 0.0) for k in range(4)]
    up = [jnp.where(row >= 7 - k, STENCIL[k], 0.0) for k in range(4)]
    for f in range(N_F):

        def y_step(x, carry):
            edge = flux(f, 1, yh[f, x], uy[x], py[x])
            total = (down[3] + up[3]) * pltpu.roll(edge, 4, 0)
            for k in range(3):
                total = total + down[k] * pltpu.roll(edge, k + 1, 0)
                total = total + up[k] * pltpu.roll(edge, 7 - k, 0)
            out[f, x, 0:8] = part[f, x, 0:8] - jnp.where(row < 4, total, zero)
            out[f, x, 8:16] = part[f, x, 8:16] - jnp.where(row < 4, zero, total)
            return carry

        lax.fori_loop(0, 16, y_step, 0, unroll=8)
        low = [flux(f, 0, xh[0, f, i], ux[0, i], px[0, i]) for i in range(4)]
        high = [flux(f, 0, xh[1, f, i], ux[1, i], px[1, i]) for i in range(4)]
        for x in range(4):
            total = None
            for k in range(x, 4):
                term = STENCIL[k] * low[3 + x - k]
                total = term if total is None else total + term
            out[f, x] += total
            total = None
            for k in range(x, 4):
                term = STENCIL[k] * high[k - x]
                total = term if total is None else total + term
            out[f, 15 - x] -= total
        copy = pltpu.make_async_copy(out.at[f], out_h.at[f], sem.at[f])
        copy.start()
        copies.append(copy)
    for copy in copies:
        copy.wait()


def shape(dims, dtype=F32):
    return jax.ShapeDtypeStruct(dims, dtype)


def per_device(n_gx, n_gy, fields, state, cell, new_cell, lists, counts):
    n_f, n_x, n_y, n_z = fields.shape
    vmem = pl.BlockSpec(memory_space=pltpu.VMEM)
    hbm = pl.BlockSpec(memory_space=pltpu.HBM)
    cube = (n_x, n_y, n_z)
    part, xh, yh, arr, own, own_cell = pl.pallas_call(
        functools.partial(droplet_kernel, n_gx, n_gy),
        out_shape=(
            shape((n_f,) + cube),
            shape((2, n_f, 4, n_y, n_z)),
            shape((n_f, n_x, 2, 4, n_z)),
            shape((4, 8, CAP)),
            shape((5, SLOTS)),
            shape((ROWS, 128), I32),
        ),
        in_specs=[hbm] * 7,
        out_specs=(vmem,) * 6,
        scratch_shapes=[
            pltpu.VMEM((n_f,) + cube, F32),
            pltpu.VMEM((ROWS, 128), I32),
            pltpu.VMEM((ROWS, 128), I32),
            pltpu.VMEM((4, CAP), I32),
            pltpu.VMEM((1, 5), I32),
            pltpu.VMEM((5, SLOTS), F32),
            pltpu.VMEM((640, 512), BF16),
            pltpu.VMEM((5, ROWS, 128), F32),
            pltpu.VMEM((10, ROWS, 128), F32),
            pltpu.VMEM((5, ROWS, 128), F32),
            pltpu.VMEM((6 * ROWS, 256), BF16),
            pltpu.VMEM((4, 8, CAP), F32),
            pltpu.VMEM((5, 128, 256), F32),
            pltpu.VMEM((3,) + cube, F32),
            pltpu.VMEM(cube, F32),
            pltpu.VMEM(cube, F32),
            pltpu.VMEM(cube, F32),
            pltpu.VMEM(cube, F32),
            pltpu.VMEM((n_x + 8, n_y, n_z), F32),
            pltpu.VMEM((n_x, n_y + 16, n_z), F32),
            pltpu.SemaphoreType.DMA((6,)),
            pltpu.SemaphoreType.DMA((8,)),
            pltpu.SemaphoreType.DMA((8,)),
        ],
        compiler_params=pltpu.CompilerParams(
            collective_id=0, has_side_effects=True, vmem_limit_bytes=36 << 20
        ),
        name="droplets",
    )(
        *(
            pltpu.with_memory_space_constraint(a, pltpu.HBM)
            for a in (
                fields,
                fields.reshape(n_f, n_x, n_y // 4, 4, n_z),
                state,
                cell.reshape(ROWS, 128),
                new_cell.reshape(ROWS, 128),
                lists,
                counts,
            )
        )
    )
    out, drops, cells = pl.pallas_call(
        edge_kernel,
        out_shape=(
            shape((n_f,) + cube),
            shape((5, SLOTS + 4 * CAP)),
            shape((ROWS + 8, 128), I32),
        ),
        in_specs=[vmem] * 6,
        out_specs=(hbm,) * 3,
        scratch_shapes=[
            pltpu.VMEM((n_f,) + cube, F32),
            pltpu.VMEM((5, SLOTS + 4 * CAP), F32),
            pltpu.VMEM((ROWS + 8, 128), I32),
            pltpu.VMEM((2, 4, n_y, n_z), F32),
            pltpu.VMEM((2, 4, n_y, n_z), F32),
            pltpu.VMEM((n_x, 8, n_z), F32),
            pltpu.VMEM((n_x, 8, n_z), F32),
            pltpu.SemaphoreType.DMA((n_f + 2,)),
        ],
        compiler_params=pltpu.CompilerParams(vmem_limit_bytes=24 << 20),
        name="edges",
    )(part, xh, yh.reshape(n_f, n_x, 8, n_z), own, own_cell, arr)
    return out, drops, cells.reshape(-1)


def solution(mesh):
    placed = (
        P(None, "gx", "gy", None),
        P(None, ("gx", "gy")),
        P(("gx", "gy")),
        P(("gx", "gy")),
        P(("gx", "gy"), None),
        P(("gx", "gy"), None),
    )
    return jax.shard_map(
        functools.partial(per_device, mesh.shape["gx"], mesh.shape["gy"]),
        mesh=mesh,
        in_specs=placed,
        out_specs=(P(None, "gx", "gy", None), P(None, ("gx", "gy")), P(("gx", "gy"))),
        check_vma=False,
    )
```

```python
import functools

import jax
import jax.numpy as jnp
from jax import lax
from jax.experimental import pallas as pl
from jax.experimental.pallas import tpu as pltpu
from jax.sharding import PartitionSpec as P

F32 = jnp.float32
BF16 = jnp.bfloat16
I32 = jnp.int32
MESH = pl.DeviceIdType.MESH

STENCIL = (1.6, -0.4, 8.0 / 105.0, -1.0 / 140.0)
SHARES = (0.0, 0.0, 0.0, 0.0, 1.5, -1.0, -2.0, 1.5, 1.5, 0.0, 0.0, 0.0, 0.0, 0.0)
N_F = 14
SLOTS = 8192
ROWS = SLOTS // 128
CAP = 256
FIRST = 7
TILE = 2048


def split(value):
    high = value.astype(BF16)
    low = (value - high.astype(F32)).astype(BF16)
    return high, low


def primitives(q):
    inverse = 1.0 / q[0]
    u = (q[1] * inverse, q[2] * inverse, q[3] * inverse)
    kinetic = 0.5 * (q[1] * q[1] + q[2] * q[2] + q[3] * q[3]) * inverse
    temper = (q[4] - kinetic) * inverse
    return inverse, u, temper, 0.4 * q[0] * temper


def evap_log(temper, q5, inverse):
    return 0.5 * jnp.log(1.0 + temper / (1.0 + q5 * inverse))


def cube_root(mass):
    return jnp.exp(jnp.log(mass) * (1.0 / 3.0))


def cell_place(c):
    column = lax.shift_left(lax.shift_right_logical(c, 14), 7) + (c & 127)
    return column, lax.shift_right_logical(c, 7) & 127


def advance(mass, theta, v, around, size):
    inverse = 1.0 / mass
    evap = size * around[4]
    heat = 0.6 * size * (around[3] - theta)
    result = [
        mass - 0.05 * evap,
        theta + 0.05 * (heat - 0.3 * evap) * inverse,
    ]
    for a in range(3):
        result.append(v[a] + 0.04 * size * (around[a] - v[a]) * inverse)
    return result


def flux(f, axis, value, u, p):
    result = u * value
    if f == axis + 1:
        result = result + p
    if f == 4:
        result = result + p * u
    return result


def droplet_kernel(
    n_gx, n_gy,
    fields, fields_y, state, cell_h, new_cell_h, lists_h, counts_h,
    part, xh, yh, arr, own, own_cell,
    fv, cell, new_cell, lists, counts, st, table, s5, sv, gas, ns, msg, dep,
    uv, pv, wv, tv, lv, fx, fy,
    in_sem, send_sem, recv_sem,
):
    gx = lax.axis_index("gx")
    gy = lax.axis_index("gy")
    x_next = (lax.rem(gx + 1, n_gx), gy)
    x_prev = (lax.rem(gx + n_gx - 1, n_gx), gy)
    y_next = (gx, lax.rem(gy + 1, n_gy))
    y_prev = (gx, lax.rem(gy + n_gy - 1, n_gy))
    targets = (x_next, x_prev, y_next, y_prev)
    barrier = pltpu.get_barrier_semaphore()
    for device in targets:
        pl.semaphore_signal(barrier, inc=1, device_id=device, device_id_type=MESH)
    loads = [
        pltpu.make_async_copy(src, dst, in_sem.at[i])
        for i, (src, dst) in enumerate(
            (
                (state, st),
                (cell_h, cell),
                (new_cell_h, new_cell),
                (lists_h, lists),
                (counts_h, counts),
                (fields, fv),
            )
        )
    ]
    for copy in loads:
        copy.start()
    n_x = fields.shape[1]
    sends = []
    for i, part_of in enumerate((slice(0, FIRST), slice(FIRST, N_F))):
        faces = (
            (fields.at[part_of, n_x - 4 : n_x], xh.at[0, part_of]),
            (fields.at[part_of, 0:4], xh.at[1, part_of]),
            (fields_y.at[part_of, :, 3], yh.at[part_of, :, 1]),
            (fields_y.at[part_of, :, 0], yh.at[part_of, :, 0]),
        )
        for j, (src, dst) in enumerate(faces):
            sends.append(
                pltpu.make_async_remote_copy(
                    src_ref=src,
                    dst_ref=dst,
                    send_sem=send_sem.at[4 * i + j],
                    recv_sem=recv_sem.at[4 * i + j],
                    device_id=targets[j],
                    device_id_type=MESH,
                )
            )
    def send_faces(first):
        y_low = lax.rem(gy, 8) == 0
        x_low = lax.rem(gx, 4) == 0
        for low, i, j in ((y_low, 3, 2), (x_low, 1, 0), (y_low, 2, 3), (x_low, 0, 1)):
            pl.when(low)(sends[first + i].start)
            pl.when(jnp.logical_not(low))(sends[first + j].start)

    def meet_and_send():
        pl.semaphore_wait(barrier, 4)
        send_faces(0)

    first_plane = lax.rem(gx, 4) == 0
    pl.when(jnp.logical_not(first_plane))(meet_and_send)
    for copy in loads:
        copy.wait()

    for i in range(ROWS):
        for k in range(5):
            s5[k, i : i + 1, :] = st[k : k + 1, i * 128 : (i + 1) * 128]
    slot = lax.broadcasted_iota(I32, (ROWS, 128), 0) * 128 + lax.broadcasted_iota(
        I32, (ROWS, 128), 1
    )
    live = slot < counts[0:1, 0:1]
    mass = s5[0]
    theta = s5[1]
    size = cube_root(mass)
    live_size = jnp.where(live, size, 0.0)
    weights = (
        live_size,
        live_size * s5[2],
        live_size * s5[3],
        live_size * s5[4],
        live_size * theta,
    )
    for k, value in enumerate(weights):
        high, low = split(value)
        sv[k] = high.astype(F32)
        sv[5 + k] = low.astype(F32)

    def cell_step(x, carry):
        q = [fv[f, x] for f in range(7)]
        inverse, u, temper, p = primitives(q)
        for a in range(3):
            uv[a, x] = u[a]
        pv[x] = p
        tv[x] = temper
        lv[x] = evap_log(temper, q[5], inverse)
        wv[x] = 20.0 * q[5] * q[6] * inverse * jnp.exp(-2.0 / temper)
        return carry

    lax.fori_loop(0, 16, cell_step, 0, unroll=2)

    for h in range(2):
        values = [v[8 * h : 8 * h + 8].reshape(128, 128) for v in (uv.at[0], uv.at[1], uv.at[2], tv, lv)]
        for k, value in enumerate(values):
            high, low = split(value)
            table[k * 128 : (k + 1) * 128, h * 128 : h * 128 + 128] = high
            table[k * 128 : (k + 1) * 128, 256 + h * 128 : 384 + h * 128] = low

    pl.when(first_plane)(meet_and_send)

    def place(values, row):
        high, low = values
        ns[row * ROWS : (row + 1) * ROWS, 0:128] = high
        ns[row * ROWS : (row + 1) * ROWS, 128:256] = low

    for k in range(5):
        place(split(s5[k]), k)
    for k, ids in ((5, new_cell[...]), (6, cell[...])):
        upper = lax.shift_left(lax.shift_right_logical(ids, 8), 8)
        place((upper.astype(F32).astype(BF16), (ids & 255).astype(F32).astype(BF16)), k)
    entry = lax.broadcasted_iota(I32, (1, CAP), 1)
    slot_rows = lax.broadcasted_iota(I32, (ROWS, CAP), 0)
    slot_lanes = lax.broadcasted_iota(I32, (128, CAP), 0)
    wide_columns = lax.broadcasted_iota(I32, (256, CAP), 0)
    wide_rows = lax.broadcasted_iota(I32, (128, CAP), 0)
    departed = jnp.zeros((ROWS, 128), F32)
    for r in range(4):
        picked = lists[r : r + 1, :]
        valid = entry < counts[0:1, 1 + r : 2 + r]
        row_mask = slot_rows == lax.shift_right_logical(picked, 7)
        lane_hot = jnp.where(slot_lanes == (picked & 127), 1.0, 0.0).astype(BF16)
        row_hot = jnp.where(row_mask & valid, 1.0, 0.0).astype(BF16)
        departed += lax.dot_general(
            row_hot, lane_hot, (((1,), (1,)), ((), ())), preferred_element_type=F32
        )
        rows = jnp.dot(
            ns[...], jnp.concatenate([lane_hot, lane_hot], 0), preferred_element_type=F32
        )
        got = [
            jnp.sum(
                jnp.where(row_mask, rows[k * ROWS : (k + 1) * ROWS], 0.0), axis=0, keepdims=True
            )
            for k in range(7)
        ]
        column, row = cell_place(got[6].astype(I32))
        hot = jnp.where(wide_columns == column, 1.0, 0.0).astype(BF16)
        rows = jnp.dot(
            table[...], jnp.concatenate([hot, hot], 0), preferred_element_type=F32
        )
        around = [
            jnp.sum(
                jnp.where(wide_rows == row, rows[k * 128 : (k + 1) * 128], 0.0),
                axis=0,
                keepdims=True,
            )
            for k in range(5)
        ]
        moved = advance(got[0], got[1], got[2:5], around, cube_root(got[0]))
        for k in range(5):
            msg[r, k : k + 1, :] = jnp.where(valid, moved[k], 0.0)
        msg[r, 5:6, :] = jnp.where(valid, got[5], -1.0)
        msg[r, 6:8, :] = jnp.zeros((2, CAP), F32)
        copy = pltpu.make_async_remote_copy(
            src_ref=msg.at[r],
            dst_ref=arr.at[r],
            send_sem=send_sem.at[8 + r],
            recv_sem=recv_sem.at[8 + r],
            device_id=targets[r],
            device_id_type=MESH,
        )
        copy.start()
        sends.append(copy)
    send_faces(4)

    per = TILE // 128
    planes = 16 * per // ROWS
    column_ids = lax.broadcasted_iota(I32, (256, 128), 0)
    row_ids = lax.broadcasted_iota(I32, (128, 128), 0)
    dep[...] = jnp.zeros_like(dep)

    def droplet_step(t, carry):
        hots = []
        masks = []
        for j in range(per):
            c = cell[pl.ds(t * per + j, 1), :]
            column, row = cell_place(c)
            hots.append(jnp.where(column_ids == column, 1.0, 0.0).astype(BF16))
            masks.append(row_ids == row)
        for j in range(0, per, 2):
            hot = jnp.concatenate(hots[j : j + 2], 1)
            rows = jnp.dot(
                table[...], jnp.concatenate([hot, hot], 0), preferred_element_type=F32
            )
            mask = jnp.concatenate(masks[j : j + 2], 1)
            for k in range(5):
                got = jnp.sum(
                    jnp.where(mask, rows[k * 128 : (k + 1) * 128], 0.0), axis=0, keepdims=True
                )
                gas[k, pl.ds(t * per + j, 1), :] = got[:, :128]
                gas[k, pl.ds(t * per + j + 1, 1), :] = got[:, 128:]
        lefts = []
        for k in range(5):
            parts = [
                jnp.where(masks[j], sv[half + k, pl.ds(t * per + j, 1), :], 0.0).astype(BF16)
                for half in (0, 5)
                for j in range(per)
            ]
            lefts.append(jnp.concatenate(parts, 1))
        sums = lax.dot_general(
            jnp.concatenate(lefts, 0),
            jnp.concatenate(hots + hots, 1),
            (((1,), (1,)), ((), ())),
            preferred_element_type=F32,
        )
        for k in range(5):
            dep[k] += sums[k * 128 : (k + 1) * 128]
        for i in range(planes):
            x = t * planes + i
            uz = uv[2, x]
            p = pv[x]
            for f in range(N_F):
                fz = flux(f, 2, fv[f, x], uz, p)
                total = None
                for k in range(4):
                    term = STENCIL[k] * (pltpu.roll(fz, 127 - k, 1) - pltpu.roll(fz, k + 1, 1))
                    total = term if total is None else total + term
                if SHARES[f] != 0.0:
                    part[f, x] = SHARES[f] * wv[x] - total
                else:
                    part[f, x] = -total
        return carry

    lax.fori_loop(0, ROWS // per, droplet_step, 0)

    new_state = advance(mass, theta, [s5[2], s5[3], s5[4]], [gas[k] for k in range(5)], size)
    staying = live & (departed == 0.0)
    own_cell[...] = jnp.where(staying, new_cell[...], -1)
    for k in range(5):
        gas[k] = jnp.where(staying, new_state[k], 0.0)
    for i in range(ROWS):
        for k in range(5):
            own[k : k + 1, i * 128 : (i + 1) * 128] = gas[k, i : i + 1, :]

    def deposit_step(x, carry):
        u = [uv[a, x] for a in range(3)]
        log = lv[x]
        rows = pl.ds(pl.multiple_of(lax.rem(x, 8) * 16, 16), 16)
        lanes = pl.ds(pl.multiple_of(lax.div(x, 8) * 128, 128), 128)
        sums = [dep[k, rows, lanes] for k in range(5)]
        evap = log * sums[0]
        part[0, x] += evap
        part[5, x] += evap
        for a in range(3):
            part[1 + a, x] += (log + 0.8) * sums[1 + a] - 0.8 * u[a] * sums[0]
        part[4, x] += (log + 0.6) * sums[4] - 0.6 * tv[x] * sums[0]
        return carry

    lax.fori_loop(0, 16, deposit_step, 0, unroll=2)
    blank = jnp.zeros((4, 16, 128), F32)
    fx[0:4] = blank
    fx[20:24] = blank
    for x in range(16):
        fy[x, 0:8] = jnp.zeros((8, 128), F32)
        fy[x, 24:32] = jnp.zeros((8, 128), F32)
    for f in range(N_F):

        def flux_step(x, carry):
            value = fv[f, x]
            fx[4 + x] = flux(f, 0, value, uv[0, x], pv[x])
            fy[x, 8:24] = flux(f, 1, value, uv[1, x], pv[x])
            return carry

        lax.fori_loop(0, 16, flux_step, 0, unroll=8)

        def rate_step(x, carry):
            total = None
            for k in range(4):
                term = (fx[x + 5 + k] - fx[x + 3 - k]) + (
                    fy[x, 9 + k : 25 + k] - fy[x, 7 - k : 23 - k]
                )
                total = STENCIL[k] * term if total is None else total + STENCIL[k] * term
            part[f, x] -= total
            return carry

        lax.fori_loop(0, 16, rate_step, 0, unroll=8)
    for copy in sends:
        copy.wait()


def edge_kernel(
    part, xh, yh, own, own_cell, arr,
    out_h, drops_h, cells_h,
    out, drops, cells, ux, px, uy, py, sem,
):
    drops[:, 0:SLOTS] = own[...]
    cells[0:ROWS, :] = own_cell[...]
    for r in range(4):
        drops[:, SLOTS + CAP * r : SLOTS + CAP * (r + 1)] = arr[r, 0:5, :]
        for j in range(2):
            row = ROWS + 2 * r + j
            cells[row : row + 1, :] = arr[r, 5:6, 128 * j : 128 * j + 128].astype(I32)
    copies = [
        pltpu.make_async_copy(drops, drops_h, sem.at[N_F]),
        pltpu.make_async_copy(cells, cells_h, sem.at[N_F + 1]),
    ]
    for copy in copies:
        copy.start()

    def cell_step(x, carry):
        _, u, _, p = primitives([yh[f, x] for f in range(5)])
        uy[x] = u[1]
        py[x] = p
        return carry

    lax.fori_loop(0, 16, cell_step, 0, unroll=4)
    for s in range(2):
        for i in range(4):
            _, u, _, p = primitives([xh[s, f, i] for f in range(5)])
            ux[s, i] = u[0]
            px[s, i] = p

    row = lax.broadcasted_iota(I32, (8, 128), 0)
    zero = jnp.zeros((8, 128), F32)
    down = [jnp.where(row < k + 1, -STENCIL[k], 0.0) for k in range(4)]
    up = [jnp.where(row >= 7 - k, STENCIL[k], 0.0) for k in range(4)]
    for f in range(N_F):

        def y_step(x, carry):
            edge = flux(f, 1, yh[f, x], uy[x], py[x])
            total = (down[3] + up[3]) * pltpu.roll(edge, 4, 0)
            for k in range(3):
                total = total + down[k] * pltpu.roll(edge, k + 1, 0)
                total = total + up[k] * pltpu.roll(edge, 7 - k, 0)
            out[f, x, 0:8] = part[f, x, 0:8] - jnp.where(row < 4, total, zero)
            out[f, x, 8:16] = part[f, x, 8:16] - jnp.where(row < 4, zero, total)
            return carry

        lax.fori_loop(0, 16, y_step, 0, unroll=8)
        low = [flux(f, 0, xh[0, f, i], ux[0, i], px[0, i]) for i in range(4)]
        high = [flux(f, 0, xh[1, f, i], ux[1, i], px[1, i]) for i in range(4)]
        for x in range(4):
            total = None
            for k in range(x, 4):
                term = STENCIL[k] * low[3 + x - k]
                total = term if total is None else total + term
            out[f, x] += total
            total = None
            for k in range(x, 4):
                term = STENCIL[k] * high[k - x]
                total = term if total is None else total + term
            out[f, 15 - x] -= total
        copy = pltpu.make_async_copy(out.at[f], out_h.at[f], sem.at[f])
        copy.start()
        copies.append(copy)
    for copy in copies:
        copy.wait()


def shape(dims, dtype=F32):
    return jax.ShapeDtypeStruct(dims, dtype)


def per_device(n_gx, n_gy, fields, state, cell, new_cell, lists, counts):
    n_f, n_x, n_y, n_z = fields.shape
    vmem = pl.BlockSpec(memory_space=pltpu.VMEM)
    hbm = pl.BlockSpec(memory_space=pltpu.HBM)
    cube = (n_x, n_y, n_z)
    part, xh, yh, arr, own, own_cell = pl.pallas_call(
        functools.partial(droplet_kernel, n_gx, n_gy),
        out_shape=(
            shape((n_f,) + cube),
            shape((2, n_f, 4, n_y, n_z)),
            shape((n_f, n_x, 2, 4, n_z)),
            shape((4, 8, CAP)),
            shape((5, SLOTS)),
            shape((ROWS, 128), I32),
        ),
        in_specs=[hbm] * 7,
        out_specs=(vmem,) * 6,
        scratch_shapes=[
            pltpu.VMEM((n_f,) + cube, F32),
            pltpu.VMEM((ROWS, 128), I32),
            pltpu.VMEM((ROWS, 128), I32),
            pltpu.VMEM((4, CAP), I32),
            pltpu.VMEM((1, 5), I32),
            pltpu.VMEM((5, SLOTS), F32),
            pltpu.VMEM((640, 512), BF16),
            pltpu.VMEM((5, ROWS, 128), F32),
            pltpu.VMEM((10, ROWS, 128), F32),
            pltpu.VMEM((5, ROWS, 128), F32),
            pltpu.VMEM((7 * ROWS, 256), BF16),
            pltpu.VMEM((4, 8, CAP), F32),
            pltpu.VMEM((5, 128, 256), F32),
            pltpu.VMEM((3,) + cube, F32),
            pltpu.VMEM(cube, F32),
            pltpu.VMEM(cube, F32),
            pltpu.VMEM(cube, F32),
            pltpu.VMEM(cube, F32),
            pltpu.VMEM((n_x + 8, n_y, n_z), F32),
            pltpu.VMEM((n_x, n_y + 16, n_z), F32),
            pltpu.SemaphoreType.DMA((6,)),
            pltpu.SemaphoreType.DMA((12,)),
            pltpu.SemaphoreType.DMA((12,)),
        ],
        compiler_params=pltpu.CompilerParams(
            collective_id=0, has_side_effects=True, vmem_limit_bytes=36 << 20
        ),
        name="droplets",
    )(
        *(
            pltpu.with_memory_space_constraint(a, pltpu.HBM)
            for a in (
                fields,
                fields.reshape(n_f, n_x, n_y // 4, 4, n_z),
                state,
                cell.reshape(ROWS, 128),
                new_cell.reshape(ROWS, 128),
                lists,
                counts,
            )
        )
    )
    out, drops, cells = pl.pallas_call(
        edge_kernel,
        out_shape=(
            shape((n_f,) + cube),
            shape((5, SLOTS + 4 * CAP)),
            shape((ROWS + 8, 128), I32),
        ),
        in_specs=[vmem] * 6,
        out_specs=(hbm,) * 3,
        scratch_shapes=[
            pltpu.VMEM((n_f,) + cube, F32),
            pltpu.VMEM((5, SLOTS + 4 * CAP), F32),
            pltpu.VMEM((ROWS + 8, 128), I32),
            pltpu.VMEM((2, 4, n_y, n_z), F32),
            pltpu.VMEM((2, 4, n_y, n_z), F32),
            pltpu.VMEM((n_x, 8, n_z), F32),
            pltpu.VMEM((n_x, 8, n_z), F32),
            pltpu.SemaphoreType.DMA((n_f + 2,)),
        ],
        compiler_params=pltpu.CompilerParams(vmem_limit_bytes=24 << 20),
        name="edges",
    )(part, xh, yh.reshape(n_f, n_x, 8, n_z), own, own_cell, arr)
    return out, drops, cells.reshape(-1)


def solution(mesh):
    placed = (
        P(None, "gx", "gy", None),
        P(None, ("gx", "gy")),
        P(("gx", "gy")),
        P(("gx", "gy")),
        P(("gx", "gy"), None),
        P(("gx", "gy"), None),
    )
    return jax.shard_map(
        functools.partial(per_device, mesh.shape["gx"], mesh.shape["gy"]),
        mesh=mesh,
        in_specs=placed,
        out_specs=(P(None, "gx", "gy", None), P(None, ("gx", "gy")), P(("gx", "gy"))),
        check_vma=False,
    )
```

```python
import functools

import jax
import jax.numpy as jnp
from jax import lax
from jax.experimental import pallas as pl
from jax.experimental.pallas import tpu as pltpu
from jax.sharding import PartitionSpec as P

F32 = jnp.float32
BF16 = jnp.bfloat16
I32 = jnp.int32
MESH = pl.DeviceIdType.MESH

STENCIL = (1.6, -0.4, 8.0 / 105.0, -1.0 / 140.0)
SHARES = (0.0, 0.0, 0.0, 0.0, 1.5, -1.0, -2.0, 1.5, 1.5, 0.0, 0.0, 0.0, 0.0, 0.0)
N_F = 14
SLOTS = 8192
ROWS = SLOTS // 128
CAP = 256
FIRST = 7
TILE = 2048


def split(value):
    high = value.astype(BF16)
    low = (value - high.astype(F32)).astype(BF16)
    return high, low


def primitives(q):
    inverse = 1.0 / q[0]
    u = (q[1] * inverse, q[2] * inverse, q[3] * inverse)
    kinetic = 0.5 * (q[1] * q[1] + q[2] * q[2] + q[3] * q[3]) * inverse
    temper = (q[4] - kinetic) * inverse
    return inverse, u, temper, 0.4 * q[0] * temper


def evap_log(temper, q5, inverse):
    return 0.5 * jnp.log(1.0 + temper / (1.0 + q5 * inverse))


def cube_root(mass):
    return jnp.exp(jnp.log(mass) * (1.0 / 3.0))


def cell_place(c):
    column = lax.shift_left(lax.shift_right_logical(c, 14), 7) + (c & 127)
    return column, lax.shift_right_logical(c, 7) & 127


def advance(mass, theta, v, around, size):
    inverse = 1.0 / mass
    evap = size * around[4]
    heat = 0.6 * size * (around[3] - theta)
    result = [
        mass - 0.05 * evap,
        theta + 0.05 * (heat - 0.3 * evap) * inverse,
    ]
    for a in range(3):
        result.append(v[a] + 0.04 * size * (around[a] - v[a]) * inverse)
    return result


def flux(f, axis, value, u, p):
    result = u * value
    if f == axis + 1:
        result = result + p
    if f == 4:
        result = result + p * u
    return result


def droplet_kernel(
    n_gx, n_gy,
    fields, fields_y, state, cell_h, new_cell_h, lists_h, counts_h,
    part, xh, yh, drops, cells,
    fv, cell, new_cell, lists, counts, st, table, s5, sv, gas, ns, msg, arr, dep,
    uv, pv, wv, tv, lv, fx, fy,
    in_sem, send_sem, recv_sem,
):
    gx = lax.axis_index("gx")
    gy = lax.axis_index("gy")
    x_next = (lax.rem(gx + 1, n_gx), gy)
    x_prev = (lax.rem(gx + n_gx - 1, n_gx), gy)
    y_next = (gx, lax.rem(gy + 1, n_gy))
    y_prev = (gx, lax.rem(gy + n_gy - 1, n_gy))
    targets = (x_next, x_prev, y_next, y_prev)
    barrier = pltpu.get_barrier_semaphore()
    for device in targets:
        pl.semaphore_signal(barrier, inc=1, device_id=device, device_id_type=MESH)
    loads = [
        pltpu.make_async_copy(src, dst, in_sem.at[i])
        for i, (src, dst) in enumerate(
            (
                (state, st),
                (cell_h, cell),
                (new_cell_h, new_cell),
                (lists_h, lists),
                (counts_h, counts),
                (fields, fv),
            )
        )
    ]
    for copy in loads:
        copy.start()
    n_x = fields.shape[1]
    sends = []
    for i, part_of in enumerate((slice(0, FIRST), slice(FIRST, N_F))):
        faces = (
            (fields.at[part_of, n_x - 4 : n_x], xh.at[0, part_of]),
            (fields.at[part_of, 0:4], xh.at[1, part_of]),
            (fields_y.at[part_of, :, 3], yh.at[part_of, :, 1]),
            (fields_y.at[part_of, :, 0], yh.at[part_of, :, 0]),
        )
        for j, (src, dst) in enumerate(faces):
            sends.append(
                pltpu.make_async_remote_copy(
                    src_ref=src,
                    dst_ref=dst,
                    send_sem=send_sem.at[4 * i + j],
                    recv_sem=recv_sem.at[4 * i + j],
                    device_id=targets[j],
                    device_id_type=MESH,
                )
            )
    plane = lax.rem(gx, 4)
    y_low = lax.rem(gy, 8) == 0

    def send_faces(batch):
        for y_first, y_second, y_is in ((3, 2, y_low), (2, 3, jnp.logical_not(y_low))):
            orders = (
                (plane == 0, ((y_first, y_first + 4, 0), (1, 5, y_second, y_second + 4, 4))),
                (plane == 3, ((0, 4, 1), (y_first, y_first + 4, y_second, y_second + 4, 5))),
                (
                    (plane == 1) | (plane == 2),
                    ((y_first, 0, y_second, 1), (y_first + 4, 4, y_second + 4, 5)),
                ),
            )
            for here, batches in orders:

                @pl.when(here & y_is)
                def _(batches=batches):
                    for i in batches[batch]:
                        sends[i].start()

    def meet_and_send():
        pl.semaphore_wait(barrier, 4)
        send_faces(0)

    first_plane = plane == 0
    pl.when(jnp.logical_not(first_plane))(meet_and_send)
    for copy in loads[:5]:
        copy.wait()

    for i in range(ROWS):
        for k in range(5):
            s5[k, i : i + 1, :] = st[k : k + 1, i * 128 : (i + 1) * 128]
    slot = lax.broadcasted_iota(I32, (ROWS, 128), 0) * 128 + lax.broadcasted_iota(
        I32, (ROWS, 128), 1
    )
    live = slot < counts[0:1, 0:1]
    mass = s5[0]
    theta = s5[1]
    size = cube_root(mass)
    live_size = jnp.where(live, size, 0.0)
    weights = (
        live_size,
        live_size * s5[2],
        live_size * s5[3],
        live_size * s5[4],
        live_size * theta,
    )
    for k, value in enumerate(weights):
        high, low = split(value)
        sv[k] = high.astype(F32)
        sv[5 + k] = low.astype(F32)

    loads[5].wait()

    def cell_step(x, carry):
        q = [fv[f, x] for f in range(7)]
        inverse, u, temper, p = primitives(q)
        for a in range(3):
            uv[a, x] = u[a]
        pv[x] = p
        tv[x] = temper
        lv[x] = evap_log(temper, q[5], inverse)
        wv[x] = 20.0 * q[5] * q[6] * inverse * jnp.exp(-2.0 / temper)
        for f in range(N_F):
            fx[f, x + 4] = flux(f, 0, fv[f, x], u[0], p)
        return carry

    for f in range(N_F):
        fx[f, 0:4] = jnp.zeros((4, 16, 128), F32)
        fx[f, 20:24] = jnp.zeros((4, 16, 128), F32)
        for i in range(fy.shape[1]):
            fy[f, i, 0:8] = jnp.zeros((8, 128), F32)
            fy[f, i, 24:32] = jnp.zeros((8, 128), F32)

    lax.fori_loop(0, 16, cell_step, 0, unroll=2)
    for h in range(2):
        values = [v[8 * h : 8 * h + 8].reshape(128, 128) for v in (uv.at[0], uv.at[1], uv.at[2], tv, lv)]
        for k, value in enumerate(values):
            high, low = split(value)
            table[k * 128 : (k + 1) * 128, h * 128 : h * 128 + 128] = high
            table[k * 128 : (k + 1) * 128, 256 + h * 128 : 384 + h * 128] = low

    pl.when(first_plane)(meet_and_send)

    def place(values, row):
        high, low = values
        ns[row * ROWS : (row + 1) * ROWS, 0:128] = high
        ns[row * ROWS : (row + 1) * ROWS, 128:256] = low

    for k in range(5):
        place(split(s5[k]), k)
    for k, ids in ((5, new_cell[...]), (6, cell[...])):
        upper = lax.shift_left(lax.shift_right_logical(ids, 8), 8)
        place((upper.astype(F32).astype(BF16), (ids & 255).astype(F32).astype(BF16)), k)
    leaving = 4 * CAP
    entry = lax.broadcasted_iota(I32, (1, CAP), 1)
    picked = jnp.concatenate([lists[r : r + 1, :] for r in range(4)], 1)
    valid = [entry < counts[0:1, 1 + r : 2 + r] for r in range(4)]
    row_mask = lax.broadcasted_iota(I32, (ROWS, leaving), 0) == lax.shift_right_logical(picked, 7)
    lane_hot = jnp.where(
        lax.broadcasted_iota(I32, (128, leaving), 0) == (picked & 127), 1.0, 0.0
    ).astype(BF16)
    row_hot = jnp.where(row_mask & jnp.concatenate(valid, 1), 1.0, 0.0).astype(BF16)
    departed = lax.dot_general(
        row_hot, lane_hot, (((1,), (1,)), ((), ())), preferred_element_type=F32
    )
    rows = jnp.dot(ns[...], jnp.concatenate([lane_hot, lane_hot], 0), preferred_element_type=F32)
    got = [
        jnp.sum(jnp.where(row_mask, rows[k * ROWS : (k + 1) * ROWS], 0.0), axis=0, keepdims=True)
        for k in range(7)
    ]
    column, row = cell_place(got[6].astype(I32))
    hot = jnp.where(
        lax.broadcasted_iota(I32, (256, leaving), 0) == column, 1.0, 0.0
    ).astype(BF16)
    rows = jnp.dot(table[...], jnp.concatenate([hot, hot], 0), preferred_element_type=F32)
    row_mask = lax.broadcasted_iota(I32, (128, leaving), 0) == row
    around = [
        jnp.sum(jnp.where(row_mask, rows[k * 128 : (k + 1) * 128], 0.0), axis=0, keepdims=True)
        for k in range(5)
    ]
    moved = advance(got[0], got[1], got[2:5], around, cube_root(got[0]))
    for r in range(4):
        lanes = slice(r * CAP, (r + 1) * CAP)
        for k in range(5):
            msg[r, k : k + 1, :] = jnp.where(valid[r], moved[k][:, lanes], 0.0)
        msg[r, 5:6, :] = jnp.where(valid[r], got[5][:, lanes], -1.0)
        msg[r, 6:8, :] = jnp.zeros((2, CAP), F32)
        copy = pltpu.make_async_remote_copy(
            src_ref=msg.at[r],
            dst_ref=arr.at[r],
            send_sem=send_sem.at[8 + r],
            recv_sem=recv_sem.at[8 + r],
            device_id=targets[r],
            device_id_type=MESH,
        )
        copy.start()
        sends.append(copy)
    send_faces(1)

    per = TILE // 128
    planes = 16 * per // ROWS
    column_ids = lax.broadcasted_iota(I32, (256, 128), 0)
    row_ids = lax.broadcasted_iota(I32, (128, 128), 0)
    dep[...] = jnp.zeros_like(dep)

    def droplet_step(t, carry):
        hots = []
        masks = []
        for j in range(per):
            c = cell[pl.ds(t * per + j, 1), :]
            column, row = cell_place(c)
            hots.append(jnp.where(column_ids == column, 1.0, 0.0).astype(BF16))
            masks.append(row_ids == row)
        for j in range(0, per, 2):
            hot = jnp.concatenate(hots[j : j + 2], 1)
            rows = jnp.dot(
                table[...], jnp.concatenate([hot, hot], 0), preferred_element_type=F32
            )
            mask = jnp.concatenate(masks[j : j + 2], 1)
            for k in range(5):
                got = jnp.sum(
                    jnp.where(mask, rows[k * 128 : (k + 1) * 128], 0.0), axis=0, keepdims=True
                )
                gas[k, pl.ds(t * per + j, 1), :] = got[:, :128]
                gas[k, pl.ds(t * per + j + 1, 1), :] = got[:, 128:]
        lefts = []
        for k in range(5):
            parts = [
                jnp.where(masks[j], sv[half + k, pl.ds(t * per + j, 1), :], 0.0).astype(BF16)
                for half in (0, 5)
                for j in range(per)
            ]
            lefts.append(jnp.concatenate(parts, 1))
        sums = lax.dot_general(
            jnp.concatenate(lefts, 0),
            jnp.concatenate(hots + hots, 1),
            (((1,), (1,)), ((), ())),
            preferred_element_type=F32,
        )
        for k in range(5):
            dep[k] += sums[k * 128 : (k + 1) * 128]
        for i in range(planes):
            x = t * planes + i
            uy = uv[1, x]
            uz = uv[2, x]
            p = pv[x]
            for f in range(N_F):
                value = fv[f, x]
                fy[f, i, 8:24] = flux(f, 1, value, uy, p)
                fz = flux(f, 2, value, uz, p)
                total = None
                for k in range(4):
                    term = STENCIL[k] * (
                        (fx[f, x + 5 + k] - fx[f, x + 3 - k])
                        + (fy[f, i, 9 + k : 25 + k] - fy[f, i, 7 - k : 23 - k])
                        + (pltpu.roll(fz, 127 - k, 1) - pltpu.roll(fz, k + 1, 1))
                    )
                    total = term if total is None else total + term
                if SHARES[f] != 0.0:
                    part[f, x] = SHARES[f] * wv[x] - total
                else:
                    part[f, x] = -total
        return carry

    lax.fori_loop(0, ROWS // per, droplet_step, 0)

    new_state = advance(mass, theta, [s5[2], s5[3], s5[4]], [gas[k] for k in range(5)], size)
    staying = live & (departed == 0.0)
    cells[0:ROWS, :] = jnp.where(staying, new_cell[...], -1)
    for k in range(5):
        gas[k] = jnp.where(staying, new_state[k], 0.0)
    for i in range(ROWS):
        for k in range(5):
            drops[k : k + 1, i * 128 : (i + 1) * 128] = gas[k, i : i + 1, :]

    def deposit_step(x, carry):
        u = [uv[a, x] for a in range(3)]
        log = lv[x]
        rows = pl.ds(pl.multiple_of(lax.rem(x, 8) * 16, 16), 16)
        lanes = pl.ds(pl.multiple_of(lax.div(x, 8) * 128, 128), 128)
        sums = [dep[k, rows, lanes] for k in range(5)]
        evap = log * sums[0]
        part[0, x] += evap
        part[5, x] += evap
        for a in range(3):
            part[1 + a, x] += (log + 0.8) * sums[1 + a] - 0.8 * u[a] * sums[0]
        part[4, x] += (log + 0.6) * sums[4] - 0.6 * tv[x] * sums[0]
        return carry

    lax.fori_loop(0, 16, deposit_step, 0, unroll=2)
    for copy in sends[8:]:
        copy.wait()
    for r in range(4):
        drops[:, SLOTS + CAP * r : SLOTS + CAP * (r + 1)] = arr[r, 0:5, :]
        for j in range(2):
            row = ROWS + 2 * r + j
            cells[row : row + 1, :] = arr[r, 5:6, 128 * j : 128 * j + 128].astype(I32)
    for copy in sends[:8]:
        copy.wait()


def edge_kernel(
    part, xh, yh, drops, cells,
    out_h, drops_h, cells_h,
    out, ux, px, uy, py, sem,
):
    copies = [
        pltpu.make_async_copy(drops, drops_h, sem.at[N_F]),
        pltpu.make_async_copy(cells, cells_h, sem.at[N_F + 1]),
    ]
    for copy in copies:
        copy.start()

    def cell_step(x, carry):
        _, u, _, p = primitives([yh[f, x] for f in range(5)])
        uy[x] = u[1]
        py[x] = p
        return carry

    lax.fori_loop(0, 16, cell_step, 0, unroll=4)
    for s in range(2):
        for i in range(4):
            _, u, _, p = primitives([xh[s, f, i] for f in range(5)])
            ux[s, i] = u[0]
            px[s, i] = p

    row = lax.broadcasted_iota(I32, (8, 128), 0)
    zero = jnp.zeros((8, 128), F32)
    down = [jnp.where(row < k + 1, -STENCIL[k], 0.0) for k in range(4)]
    up = [jnp.where(row >= 7 - k, STENCIL[k], 0.0) for k in range(4)]
    for f in range(N_F):

        def y_step(x, carry):
            edge = flux(f, 1, yh[f, x], uy[x], py[x])
            total = (down[3] + up[3]) * pltpu.roll(edge, 4, 0)
            for k in range(3):
                total = total + down[k] * pltpu.roll(edge, k + 1, 0)
                total = total + up[k] * pltpu.roll(edge, 7 - k, 0)
            out[f, x, 0:8] = part[f, x, 0:8] - jnp.where(row < 4, total, zero)
            out[f, x, 8:16] = part[f, x, 8:16] - jnp.where(row < 4, zero, total)
            return carry

        lax.fori_loop(0, 16, y_step, 0, unroll=8)
        low = [flux(f, 0, xh[0, f, i], ux[0, i], px[0, i]) for i in range(4)]
        high = [flux(f, 0, xh[1, f, i], ux[1, i], px[1, i]) for i in range(4)]
        for x in range(4):
            total = None
            for k in range(x, 4):
                term = STENCIL[k] * low[3 + x - k]
                total = term if total is None else total + term
            out[f, x] += total
            total = None
            for k in range(x, 4):
                term = STENCIL[k] * high[k - x]
                total = term if total is None else total + term
            out[f, 15 - x] -= total
        copy = pltpu.make_async_copy(out.at[f], out_h.at[f], sem.at[f])
        copy.start()
        copies.append(copy)
    for copy in copies:
        copy.wait()


def shape(dims, dtype=F32):
    return jax.ShapeDtypeStruct(dims, dtype)


def per_device(n_gx, n_gy, fields, state, cell, new_cell, lists, counts):
    n_f, n_x, n_y, n_z = fields.shape
    vmem = pl.BlockSpec(memory_space=pltpu.VMEM)
    hbm = pl.BlockSpec(memory_space=pltpu.HBM)
    cube = (n_x, n_y, n_z)
    part, xh, yh, drops, cells = pl.pallas_call(
        functools.partial(droplet_kernel, n_gx, n_gy),
        out_shape=(
            shape((n_f,) + cube),
            shape((2, n_f, 4, n_y, n_z)),
            shape((n_f, n_x, 2, 4, n_z)),
            shape((5, SLOTS + 4 * CAP)),
            shape((ROWS + 8, 128), I32),
        ),
        in_specs=[hbm] * 7,
        out_specs=(vmem,) * 5,
        scratch_shapes=[
            pltpu.VMEM((n_f,) + cube, F32),
            pltpu.VMEM((ROWS, 128), I32),
            pltpu.VMEM((ROWS, 128), I32),
            pltpu.VMEM((4, CAP), I32),
            pltpu.VMEM((1, 5), I32),
            pltpu.VMEM((5, SLOTS), F32),
            pltpu.VMEM((640, 512), BF16),
            pltpu.VMEM((5, ROWS, 128), F32),
            pltpu.VMEM((10, ROWS, 128), F32),
            pltpu.VMEM((5, ROWS, 128), F32),
            pltpu.VMEM((7 * ROWS, 256), BF16),
            pltpu.VMEM((4, 8, CAP), F32),
            pltpu.VMEM((4, 8, CAP), F32),
            pltpu.VMEM((5, 128, 256), F32),
            pltpu.VMEM((3,) + cube, F32),
            pltpu.VMEM(cube, F32),
            pltpu.VMEM(cube, F32),
            pltpu.VMEM(cube, F32),
            pltpu.VMEM(cube, F32),
            pltpu.VMEM((n_f, n_x + 8, n_y, n_z), F32),
            pltpu.VMEM((n_f, n_x * TILE // SLOTS, n_y + 16, n_z), F32),
            pltpu.SemaphoreType.DMA((6,)),
            pltpu.SemaphoreType.DMA((12,)),
            pltpu.SemaphoreType.DMA((12,)),
        ],
        compiler_params=pltpu.CompilerParams(
            collective_id=0, has_side_effects=True, vmem_limit_bytes=36 << 20
        ),
        name="droplets",
    )(
        *(
            pltpu.with_memory_space_constraint(a, pltpu.HBM)
            for a in (
                fields,
                fields.reshape(n_f, n_x, n_y // 4, 4, n_z),
                state,
                cell.reshape(ROWS, 128),
                new_cell.reshape(ROWS, 128),
                lists,
                counts,
            )
        )
    )
    out, drops, cells = pl.pallas_call(
        edge_kernel,
        out_shape=(
            shape((n_f,) + cube),
            shape((5, SLOTS + 4 * CAP)),
            shape((ROWS + 8, 128), I32),
        ),
        in_specs=[vmem] * 5,
        out_specs=(hbm,) * 3,
        scratch_shapes=[
            pltpu.VMEM((n_f,) + cube, F32),
            pltpu.VMEM((2, 4, n_y, n_z), F32),
            pltpu.VMEM((2, 4, n_y, n_z), F32),
            pltpu.VMEM((n_x, 8, n_z), F32),
            pltpu.VMEM((n_x, 8, n_z), F32),
            pltpu.SemaphoreType.DMA((n_f + 2,)),
        ],
        compiler_params=pltpu.CompilerParams(vmem_limit_bytes=24 << 20),
        name="edges",
    )(part, xh, yh.reshape(n_f, n_x, 8, n_z), drops, cells)
    return out, drops, cells.reshape(-1)


def solution(mesh):
    placed = (
        P(None, "gx", "gy", None),
        P(None, ("gx", "gy")),
        P(("gx", "gy")),
        P(("gx", "gy")),
        P(("gx", "gy"), None),
        P(("gx", "gy"), None),
    )
    return jax.shard_map(
        functools.partial(per_device, mesh.shape["gx"], mesh.shape["gy"]),
        mesh=mesh,
        in_specs=placed,
        out_specs=(P(None, "gx", "gy", None), P(None, ("gx", "gy")), P(("gx", "gy"))),
        check_vma=False,
    )
```

```python
import functools

import jax
import jax.numpy as jnp
from jax import lax
from jax.experimental import pallas as pl
from jax.experimental.pallas import tpu as pltpu
from jax.sharding import PartitionSpec as P

F32 = jnp.float32
BF16 = jnp.bfloat16
I32 = jnp.int32
MESH = pl.DeviceIdType.MESH

STENCIL = (1.6, -0.4, 8.0 / 105.0, -1.0 / 140.0)
SHARES = (0.0, 0.0, 0.0, 0.0, 1.5, -1.0, -2.0, 1.5, 1.5, 0.0, 0.0, 0.0, 0.0, 0.0)
N_F = 14
SLOTS = 8192
ROWS = SLOTS // 128
CAP = 256
FIRST = 7
TILE = 2048


def split(value):
    high = value.astype(BF16)
    low = (value - high.astype(F32)).astype(BF16)
    return high, low


def primitives(q):
    inverse = 1.0 / q[0]
    u = (q[1] * inverse, q[2] * inverse, q[3] * inverse)
    kinetic = 0.5 * (q[1] * q[1] + q[2] * q[2] + q[3] * q[3]) * inverse
    temper = (q[4] - kinetic) * inverse
    return inverse, u, temper, 0.4 * q[0] * temper


def evap_log(temper, q5, inverse):
    return 0.5 * jnp.log(1.0 + temper / (1.0 + q5 * inverse))


def cube_root(mass):
    return jnp.exp(jnp.log(mass) * (1.0 / 3.0))


def cell_place(c):
    column = lax.shift_left(lax.shift_right_logical(c, 14), 7) + (c & 127)
    return column, lax.shift_right_logical(c, 7) & 127


def advance(mass, theta, v, around, size):
    inverse = 1.0 / mass
    evap = size * around[4]
    heat = 0.6 * size * (around[3] - theta)
    result = [
        mass - 0.05 * evap,
        theta + 0.05 * (heat - 0.3 * evap) * inverse,
    ]
    for a in range(3):
        result.append(v[a] + 0.04 * size * (around[a] - v[a]) * inverse)
    return result


def flux(f, axis, value, u, p):
    result = u * value
    if f == axis + 1:
        result = result + p
    if f == 4:
        result = result + p * u
    return result


def droplet_kernel(
    n_gx, n_gy,
    fields, fields_y, state, cell_h, new_cell_h, lists_h, counts_h,
    part, xh, yh, drops, cells,
    fv, cell, new_cell, lists, counts, st, table, s5, sv, gas, ns, msg, arr, dep,
    uv, pv, wv, tv, lv, fx, fy,
    in_sem, send_sem, recv_sem,
):
    gx = lax.axis_index("gx")
    gy = lax.axis_index("gy")
    x_next = (lax.rem(gx + 1, n_gx), gy)
    x_prev = (lax.rem(gx + n_gx - 1, n_gx), gy)
    y_next = (gx, lax.rem(gy + 1, n_gy))
    y_prev = (gx, lax.rem(gy + n_gy - 1, n_gy))
    targets = (x_next, x_prev, y_next, y_prev)
    barrier = pltpu.get_barrier_semaphore()
    for device in targets:
        pl.semaphore_signal(barrier, inc=1, device_id=device, device_id_type=MESH)
    loads = [
        pltpu.make_async_copy(src, dst, in_sem.at[i])
        for i, (src, dst) in enumerate(
            (
                (state, st),
                (cell_h, cell),
                (new_cell_h, new_cell),
                (lists_h, lists),
                (counts_h, counts),
                (fields, fv),
            )
        )
    ]
    for copy in loads:
        copy.start()
    n_x = fields.shape[1]
    sends = []
    for i, part_of in enumerate((slice(0, FIRST), slice(FIRST, N_F))):
        faces = (
            (fields.at[part_of, n_x - 4 : n_x], xh.at[0, part_of]),
            (fields.at[part_of, 0:4], xh.at[1, part_of]),
            (fields_y.at[part_of, :, 3], yh.at[part_of, :, 1]),
            (fields_y.at[part_of, :, 0], yh.at[part_of, :, 0]),
        )
        for j, (src, dst) in enumerate(faces):
            sends.append(
                pltpu.make_async_remote_copy(
                    src_ref=src,
                    dst_ref=dst,
                    send_sem=send_sem.at[4 * i + j],
                    recv_sem=recv_sem.at[4 * i + j],
                    device_id=targets[j],
                    device_id_type=MESH,
                )
            )
    plane = lax.rem(gx, 4)
    y_low = lax.rem(gy, 8) == 0

    def send_faces(batch):
        for y_first, y_second, y_is in ((3, 2, y_low), (2, 3, jnp.logical_not(y_low))):
            orders = (
                (plane == 0, ((y_first, y_first + 4, 0), (1, 5, y_second, y_second + 4, 4))),
                (plane == 3, ((0, 4, 1), (y_first, y_first + 4, y_second, y_second + 4, 5))),
                (
                    (plane == 1) | (plane == 2),
                    ((y_first, 0, y_second, 1), (y_first + 4, 4, y_second + 4, 5)),
                ),
            )
            for here, batches in orders:

                @pl.when(here & y_is)
                def _(batches=batches):
                    for i in batches[batch]:
                        sends[i].start()

    def meet_and_send():
        pl.semaphore_wait(barrier, 4)
        send_faces(0)

    first_plane = plane == 0
    pl.when(jnp.logical_not(first_plane))(meet_and_send)
    for copy in loads[:5]:
        copy.wait()

    for i in range(ROWS):
        for k in range(5):
            s5[k, i : i + 1, :] = st[k : k + 1, i * 128 : (i + 1) * 128]
    slot = lax.broadcasted_iota(I32, (ROWS, 128), 0) * 128 + lax.broadcasted_iota(
        I32, (ROWS, 128), 1
    )
    live = slot < counts[0:1, 0:1]
    mass = s5[0]
    theta = s5[1]
    size = cube_root(mass)
    live_size = jnp.where(live, size, 0.0)
    weights = (
        live_size,
        live_size * s5[2],
        live_size * s5[3],
        live_size * s5[4],
        live_size * theta,
    )
    for k, value in enumerate(weights):
        high, low = split(value)
        sv[k] = high.astype(F32)
        sv[5 + k] = low.astype(F32)

    loads[5].wait()

    def cell_step(x, carry):
        q = [fv[f, x] for f in range(7)]
        inverse, u, temper, p = primitives(q)
        for a in range(3):
            uv[a, x] = u[a]
        pv[x] = p
        tv[x] = temper
        lv[x] = evap_log(temper, q[5], inverse)
        wv[x] = 20.0 * q[5] * q[6] * inverse * jnp.exp(-2.0 / temper)
        for f in range(N_F):
            fx[f, x + 4] = flux(f, 0, fv[f, x], u[0], p)
        return carry

    for f in range(N_F):
        fx[f, 0:4] = jnp.zeros((4, 16, 128), F32)
        fx[f, 20:24] = jnp.zeros((4, 16, 128), F32)
        for i in range(fy.shape[1]):
            fy[f, i, 0:8] = jnp.zeros((8, 128), F32)
            fy[f, i, 24:32] = jnp.zeros((8, 128), F32)

    lax.fori_loop(0, 16, cell_step, 0, unroll=2)
    for h in range(2):
        values = [v[8 * h : 8 * h + 8].reshape(128, 128) for v in (uv.at[0], uv.at[1], uv.at[2], tv, lv)]
        for k, value in enumerate(values):
            high, low = split(value)
            table[k * 128 : (k + 1) * 128, h * 128 : h * 128 + 128] = high
            table[k * 128 : (k + 1) * 128, 256 + h * 128 : 384 + h * 128] = low

    pl.when(first_plane)(meet_and_send)

    def place(values, row):
        high, low = values
        ns[row * ROWS : (row + 1) * ROWS, 0:128] = high
        ns[row * ROWS : (row + 1) * ROWS, 128:256] = low

    for k in range(5):
        place(split(s5[k]), k)
    for k, ids in ((5, new_cell[...]), (6, cell[...])):
        upper = lax.shift_left(lax.shift_right_logical(ids, 8), 8)
        place((upper.astype(F32).astype(BF16), (ids & 255).astype(F32).astype(BF16)), k)
    leaving = 4 * CAP
    entry = lax.broadcasted_iota(I32, (1, CAP), 1)
    picked = jnp.concatenate([lists[r : r + 1, :] for r in range(4)], 1)
    valid = [entry < counts[0:1, 1 + r : 2 + r] for r in range(4)]
    row_mask = lax.broadcasted_iota(I32, (ROWS, leaving), 0) == lax.shift_right_logical(picked, 7)
    lane_hot = jnp.where(
        lax.broadcasted_iota(I32, (128, leaving), 0) == (picked & 127), 1.0, 0.0
    ).astype(BF16)
    row_hot = jnp.where(row_mask & jnp.concatenate(valid, 1), 1.0, 0.0).astype(BF16)
    departed = lax.dot_general(
        row_hot, lane_hot, (((1,), (1,)), ((), ())), preferred_element_type=F32
    )
    rows = jnp.dot(ns[...], jnp.concatenate([lane_hot, lane_hot], 0), preferred_element_type=F32)
    got = [
        jnp.sum(jnp.where(row_mask, rows[k * ROWS : (k + 1) * ROWS], 0.0), axis=0, keepdims=True)
        for k in range(7)
    ]
    column, row = cell_place(got[6].astype(I32))
    hot = jnp.where(
        lax.broadcasted_iota(I32, (256, leaving), 0) == column, 1.0, 0.0
    ).astype(BF16)
    rows = jnp.dot(table[...], jnp.concatenate([hot, hot], 0), preferred_element_type=F32)
    row_mask = lax.broadcasted_iota(I32, (128, leaving), 0) == row
    around = [
        jnp.sum(jnp.where(row_mask, rows[k * 128 : (k + 1) * 128], 0.0), axis=0, keepdims=True)
        for k in range(5)
    ]
    moved = advance(got[0], got[1], got[2:5], around, cube_root(got[0]))
    for r in range(4):
        lanes = slice(r * CAP, (r + 1) * CAP)
        for k in range(5):
            msg[r, k : k + 1, :] = jnp.where(valid[r], moved[k][:, lanes], 0.0)
        msg[r, 5:6, :] = jnp.where(valid[r], got[5][:, lanes], -1.0)
        msg[r, 6:8, :] = jnp.zeros((2, CAP), F32)
        copy = pltpu.make_async_remote_copy(
            src_ref=msg.at[r],
            dst_ref=arr.at[r],
            send_sem=send_sem.at[8 + r],
            recv_sem=recv_sem.at[8 + r],
            device_id=targets[r],
            device_id_type=MESH,
        )
        copy.start()
        sends.append(copy)
    send_faces(1)

    per = TILE // 128
    planes = 16 * per // ROWS
    column_ids = lax.broadcasted_iota(I32, (256, 128), 0)
    row_ids = lax.broadcasted_iota(I32, (128, 128), 0)
    dep[...] = jnp.zeros_like(dep)

    def droplet_step(t, carry):
        hots = []
        masks = []
        for j in range(per):
            c = cell[pl.ds(t * per + j, 1), :]
            column, row = cell_place(c)
            hots.append(jnp.where(column_ids == column, 1.0, 0.0).astype(BF16))
            masks.append(row_ids == row)
        for j in range(0, per, 2):
            hot = jnp.concatenate(hots[j : j + 2], 1)
            rows = jnp.dot(
                table[...], jnp.concatenate([hot, hot], 0), preferred_element_type=F32
            )
            mask = jnp.concatenate(masks[j : j + 2], 1)
            for k in range(5):
                got = jnp.sum(
                    jnp.where(mask, rows[k * 128 : (k + 1) * 128], 0.0), axis=0, keepdims=True
                )
                gas[k, pl.ds(t * per + j, 1), :] = got[:, :128]
                gas[k, pl.ds(t * per + j + 1, 1), :] = got[:, 128:]
        lefts = []
        for k in range(5):
            parts = [
                jnp.where(masks[j], sv[half + k, pl.ds(t * per + j, 1), :], 0.0).astype(BF16)
                for half in (0, 5)
                for j in range(per)
            ]
            lefts.append(jnp.concatenate(parts, 1))
        sums = lax.dot_general(
            jnp.concatenate(lefts, 0),
            jnp.concatenate(hots + hots, 1),
            (((1,), (1,)), ((), ())),
            preferred_element_type=F32,
        )
        for k in range(5):
            dep[k] += sums[k * 128 : (k + 1) * 128]
        for i in range(planes):
            x = t * planes + i
            uy = uv[1, x]
            uz = uv[2, x]
            p = pv[x]
            for f in range(N_F):
                value = fv[f, x]
                fy[f, i, 8:24] = flux(f, 1, value, uy, p)
                fz = flux(f, 2, value, uz, p)
                total = None
                for k in range(4):
                    term = STENCIL[k] * (
                        (fx[f, x + 5 + k] - fx[f, x + 3 - k])
                        + (fy[f, i, 9 + k : 25 + k] - fy[f, i, 7 - k : 23 - k])
                        + (pltpu.roll(fz, 127 - k, 1) - pltpu.roll(fz, k + 1, 1))
                    )
                    total = term if total is None else total + term
                if SHARES[f] != 0.0:
                    part[f, x] = SHARES[f] * wv[x] - total
                else:
                    part[f, x] = -total
        return carry

    lax.fori_loop(0, ROWS // per, droplet_step, 0)

    new_state = advance(mass, theta, [s5[2], s5[3], s5[4]], [gas[k] for k in range(5)], size)
    staying = live & (departed == 0.0)
    cells[0:ROWS, :] = jnp.where(staying, new_cell[...], -1)
    for k in range(5):
        gas[k] = jnp.where(staying, new_state[k], 0.0)
    for i in range(ROWS):
        for k in range(5):
            drops[k : k + 1, i * 128 : (i + 1) * 128] = gas[k, i : i + 1, :]

    def deposit_step(x, carry):
        u = [uv[a, x] for a in range(3)]
        log = lv[x]
        rows = pl.ds(pl.multiple_of(lax.rem(x, 8) * 16, 16), 16)
        lanes = pl.ds(pl.multiple_of(lax.div(x, 8) * 128, 128), 128)
        sums = [dep[k, rows, lanes] for k in range(5)]
        evap = log * sums[0]
        part[0, x] += evap
        part[5, x] += evap
        for a in range(3):
            part[1 + a, x] += (log + 0.8) * sums[1 + a] - 0.8 * u[a] * sums[0]
        part[4, x] += (log + 0.6) * sums[4] - 0.6 * tv[x] * sums[0]
        return carry

    lax.fori_loop(0, 16, deposit_step, 0, unroll=2)
    for copy in sends[8:]:
        copy.wait()
    for r in range(4):
        drops[:, SLOTS + CAP * r : SLOTS + CAP * (r + 1)] = arr[r, 0:5, :]
        for j in range(2):
            row = ROWS + 2 * r + j
            cells[row : row + 1, :] = arr[r, 5:6, 128 * j : 128 * j + 128].astype(I32)
    for copy in sends[:8]:
        copy.wait()


def edge_kernel(
    part, xh, yh, drops, cells,
    out_h, drops_h, cells_h,
    out, ux, px, uy, py, fy, sem,
):
    copies = [
        pltpu.make_async_copy(drops, drops_h, sem.at[N_F]),
        pltpu.make_async_copy(cells, cells_h, sem.at[N_F + 1]),
    ]
    for copy in copies:
        copy.start()

    def cell_step(x, carry):
        _, u, _, p = primitives([yh[f, x] for f in range(5)])
        uy[x] = u[1]
        py[x] = p
        return carry

    lax.fori_loop(0, 16, cell_step, 0, unroll=16)
    for s in range(2):
        for i in range(4):
            _, u, _, p = primitives([xh[s, f, i] for f in range(5)])
            ux[s, i] = u[0]
            px[s, i] = p

    for x in range(16):
        fy[x, 8:24] = jnp.zeros((16, 128), F32)
    for f in range(N_F):

        def y_step(x, carry):
            edge = flux(f, 1, yh[f, x], uy[x], py[x])
            fy[x, 0:8] = edge
            fy[x, 24:32] = edge
            low = None
            high = None
            for k in range(4):
                term = STENCIL[k] * fy[x, 7 - k : 15 - k]
                low = term if low is None else low + term
                term = STENCIL[k] * fy[x, 17 + k : 25 + k]
                high = term if high is None else high + term
            out[f, x, 0:8] = part[f, x, 0:8] + low
            out[f, x, 8:16] = part[f, x, 8:16] - high
            return carry

        lax.fori_loop(0, 16, y_step, 0, unroll=16)
        low = [flux(f, 0, xh[0, f, i], ux[0, i], px[0, i]) for i in range(4)]
        high = [flux(f, 0, xh[1, f, i], ux[1, i], px[1, i]) for i in range(4)]
        for x in range(4):
            total = None
            for k in range(x, 4):
                term = STENCIL[k] * low[3 + x - k]
                total = term if total is None else total + term
            out[f, x] += total
            total = None
            for k in range(x, 4):
                term = STENCIL[k] * high[k - x]
                total = term if total is None else total + term
            out[f, 15 - x] -= total
        copy = pltpu.make_async_copy(out.at[f], out_h.at[f], sem.at[f])
        copy.start()
        copies.append(copy)
    for copy in copies:
        copy.wait()


def shape(dims, dtype=F32):
    return jax.ShapeDtypeStruct(dims, dtype)


def per_device(n_gx, n_gy, fields, state, cell, new_cell, lists, counts):
    n_f, n_x, n_y, n_z = fields.shape
    vmem = pl.BlockSpec(memory_space=pltpu.VMEM)
    hbm = pl.BlockSpec(memory_space=pltpu.HBM)
    cube = (n_x, n_y, n_z)
    part, xh, yh, drops, cells = pl.pallas_call(
        functools.partial(droplet_kernel, n_gx, n_gy),
        out_shape=(
            shape((n_f,) + cube),
            shape((2, n_f, 4, n_y, n_z)),
            shape((n_f, n_x, 2, 4, n_z)),
            shape((5, SLOTS + 4 * CAP)),
            shape((ROWS + 8, 128), I32),
        ),
        in_specs=[hbm] * 7,
        out_specs=(vmem,) * 5,
        scratch_shapes=[
            pltpu.VMEM((n_f,) + cube, F32),
            pltpu.VMEM((ROWS, 128), I32),
            pltpu.VMEM((ROWS, 128), I32),
            pltpu.VMEM((4, CAP), I32),
            pltpu.VMEM((1, 5), I32),
            pltpu.VMEM((5, SLOTS), F32),
            pltpu.VMEM((640, 512), BF16),
            pltpu.VMEM((5, ROWS, 128), F32),
            pltpu.VMEM((10, ROWS, 128), F32),
            pltpu.VMEM((5, ROWS, 128), F32),
            pltpu.VMEM((7 * ROWS, 256), BF16),
            pltpu.VMEM((4, 8, CAP), F32),
            pltpu.VMEM((4, 8, CAP), F32),
            pltpu.VMEM((5, 128, 256), F32),
            pltpu.VMEM((3,) + cube, F32),
            pltpu.VMEM(cube, F32),
            pltpu.VMEM(cube, F32),
            pltpu.VMEM(cube, F32),
            pltpu.VMEM(cube, F32),
            pltpu.VMEM((n_f, n_x + 8, n_y, n_z), F32),
            pltpu.VMEM((n_f, n_x * TILE // SLOTS, n_y + 16, n_z), F32),
            pltpu.SemaphoreType.DMA((6,)),
            pltpu.SemaphoreType.DMA((12,)),
            pltpu.SemaphoreType.DMA((12,)),
        ],
        compiler_params=pltpu.CompilerParams(
            collective_id=0, has_side_effects=True, vmem_limit_bytes=36 << 20
        ),
        name="droplets",
    )(
        *(
            pltpu.with_memory_space_constraint(a, pltpu.HBM)
            for a in (
                fields,
                fields.reshape(n_f, n_x, n_y // 4, 4, n_z),
                state,
                cell.reshape(ROWS, 128),
                new_cell.reshape(ROWS, 128),
                lists,
                counts,
            )
        )
    )
    out, drops, cells = pl.pallas_call(
        edge_kernel,
        out_shape=(
            shape((n_f,) + cube),
            shape((5, SLOTS + 4 * CAP)),
            shape((ROWS + 8, 128), I32),
        ),
        in_specs=[vmem] * 5,
        out_specs=(hbm,) * 3,
        scratch_shapes=[
            pltpu.VMEM((n_f,) + cube, F32),
            pltpu.VMEM((2, 4, n_y, n_z), F32),
            pltpu.VMEM((2, 4, n_y, n_z), F32),
            pltpu.VMEM((n_x, 8, n_z), F32),
            pltpu.VMEM((n_x, 8, n_z), F32),
            pltpu.VMEM((n_x, n_y + 16, n_z), F32),
            pltpu.SemaphoreType.DMA((n_f + 2,)),
        ],
        compiler_params=pltpu.CompilerParams(vmem_limit_bytes=24 << 20),
        name="edges",
    )(part, xh, yh.reshape(n_f, n_x, 8, n_z), drops, cells)
    return out, drops, cells.reshape(-1)


def solution(mesh):
    placed = (
        P(None, "gx", "gy", None),
        P(None, ("gx", "gy")),
        P(("gx", "gy")),
        P(("gx", "gy")),
        P(("gx", "gy"), None),
        P(("gx", "gy"), None),
    )
    return jax.shard_map(
        functools.partial(per_device, mesh.shape["gx"], mesh.shape["gy"]),
        mesh=mesh,
        in_specs=placed,
        out_specs=(P(None, "gx", "gy", None), P(None, ("gx", "gy")), P(("gx", "gy"))),
        check_vma=False,
    )
```

```python
import functools

import jax
import jax.numpy as jnp
from jax import lax
from jax.experimental import pallas as pl
from jax.experimental.pallas import tpu as pltpu
from jax.sharding import PartitionSpec as P

F32 = jnp.float32
BF16 = jnp.bfloat16
I32 = jnp.int32
MESH = pl.DeviceIdType.MESH

STENCIL = (1.6, -0.4, 8.0 / 105.0, -1.0 / 140.0)
SHARES = (0.0, 0.0, 0.0, 0.0, 1.5, -1.0, -2.0, 1.5, 1.5, 0.0, 0.0, 0.0, 0.0, 0.0)
N_F = 14
SLOTS = 8192
ROWS = SLOTS // 128
CAP = 256
FIRST = 7
TILE = 2048


def split(value):
    high = value.astype(BF16)
    low = (value - high.astype(F32)).astype(BF16)
    return high, low


def primitives(q):
    inverse = 1.0 / q[0]
    u = (q[1] * inverse, q[2] * inverse, q[3] * inverse)
    kinetic = 0.5 * (q[1] * q[1] + q[2] * q[2] + q[3] * q[3]) * inverse
    temper = (q[4] - kinetic) * inverse
    return inverse, u, temper, 0.4 * q[0] * temper


def evap_log(temper, q5, inverse):
    return 0.5 * jnp.log(1.0 + temper / (1.0 + q5 * inverse))


def cube_root(mass):
    return jnp.exp(jnp.log(mass) * (1.0 / 3.0))


def cell_place(c):
    column = lax.shift_left(lax.shift_right_logical(c, 14), 7) + (c & 127)
    return column, lax.shift_right_logical(c, 7) & 127


def advance(mass, theta, v, around, size):
    inverse = 1.0 / mass
    evap = size * around[4]
    heat = 0.6 * size * (around[3] - theta)
    result = [
        mass - 0.05 * evap,
        theta + 0.05 * (heat - 0.3 * evap) * inverse,
    ]
    for a in range(3):
        result.append(v[a] + 0.04 * size * (around[a] - v[a]) * inverse)
    return result


def flux(f, axis, value, u, p):
    result = u * value
    if f == axis + 1:
        result = result + p
    if f == 4:
        result = result + p * u
    return result


def droplet_kernel(
    n_gx, n_gy,
    fields, fields_y, state, cell_h, new_cell_h, lists_h, counts_h,
    part, xh, yh, drops, cells,
    fv, cell, new_cell, lists, counts, st, table, s5, sv, gas, ns, msg, arr, dep,
    uv, pv, wv, tv, lv, fx, fy,
    in_sem, send_sem, recv_sem,
):
    gx = lax.axis_index("gx")
    gy = lax.axis_index("gy")
    x_next = (lax.rem(gx + 1, n_gx), gy)
    x_prev = (lax.rem(gx + n_gx - 1, n_gx), gy)
    y_next = (gx, lax.rem(gy + 1, n_gy))
    y_prev = (gx, lax.rem(gy + n_gy - 1, n_gy))
    targets = (x_next, x_prev, y_next, y_prev)
    barrier = pltpu.get_barrier_semaphore()
    for device in targets:
        pl.semaphore_signal(barrier, inc=1, device_id=device, device_id_type=MESH)
    loads = [
        pltpu.make_async_copy(src, dst, in_sem.at[i])
        for i, (src, dst) in enumerate(
            (
                (state, st),
                (cell_h, cell),
                (new_cell_h, new_cell),
                (lists_h, lists),
                (counts_h, counts),
                (fields, fv),
            )
        )
    ]
    for copy in loads:
        copy.start()
    n_x = fields.shape[1]
    sends = []
    for i, part_of in enumerate((slice(0, FIRST), slice(FIRST, N_F))):
        faces = (
            (fields.at[part_of, n_x - 4 : n_x], xh.at[0, part_of]),
            (fields.at[part_of, 0:4], xh.at[1, part_of]),
            (fields_y.at[part_of, :, 3], yh.at[part_of, :, 1]),
            (fields_y.at[part_of, :, 0], yh.at[part_of, :, 0]),
        )
        for j, (src, dst) in enumerate(faces):
            sends.append(
                pltpu.make_async_remote_copy(
                    src_ref=src,
                    dst_ref=dst,
                    send_sem=send_sem.at[4 * i + j],
                    recv_sem=recv_sem.at[4 * i + j],
                    device_id=targets[j],
                    device_id_type=MESH,
                )
            )
    plane = lax.rem(gx, 4)
    y_low = lax.rem(gy, 8) == 0

    def send_faces(batch):
        for y_first, y_second, y_is in ((3, 2, y_low), (2, 3, jnp.logical_not(y_low))):
            orders = (
                (plane == 0, ((y_first, y_first + 4, 0), (1, 5, y_second, y_second + 4, 4))),
                (plane == 3, ((0, 4, 1), (y_first, y_first + 4, y_second, y_second + 4, 5))),
                (
                    (plane == 1) | (plane == 2),
                    ((y_first, 0, y_second, 1), (y_first + 4, 4, y_second + 4, 5)),
                ),
            )
            for here, batches in orders:

                @pl.when(here & y_is)
                def _(batches=batches):
                    for i in batches[batch]:
                        sends[i].start()

    def meet_and_send():
        pl.semaphore_wait(barrier, 4)
        send_faces(0)

    first_plane = plane == 0
    pl.when(jnp.logical_not(first_plane))(meet_and_send)
    for copy in loads[:5]:
        copy.wait()

    for i in range(ROWS):
        for k in range(5):
            s5[k, i : i + 1, :] = st[k : k + 1, i * 128 : (i + 1) * 128]
    slot = lax.broadcasted_iota(I32, (ROWS, 128), 0) * 128 + lax.broadcasted_iota(
        I32, (ROWS, 128), 1
    )
    live = slot < counts[0:1, 0:1]
    mass = s5[0]
    theta = s5[1]
    size = cube_root(mass)
    live_size = jnp.where(live, size, 0.0)
    weights = (
        live_size,
        live_size * s5[2],
        live_size * s5[3],
        live_size * s5[4],
        live_size * theta,
    )
    for k, value in enumerate(weights):
        high, low = split(value)
        sv[k] = high.astype(F32)
        sv[5 + k] = low.astype(F32)

    loads[5].wait()

    def cell_step(x, carry):
        q = [fv[f, x] for f in range(7)]
        inverse, u, temper, p = primitives(q)
        for a in range(3):
            uv[a, x] = u[a]
        pv[x] = p
        tv[x] = temper
        lv[x] = evap_log(temper, q[5], inverse)
        wv[x] = 20.0 * q[5] * q[6] * inverse * jnp.exp(-2.0 / temper)
        for f in range(N_F):
            fx[f, x + 4] = flux(f, 0, fv[f, x], u[0], p)
        return carry

    for f in range(N_F):
        fx[f, 0:4] = jnp.zeros((4, 16, 128), F32)
        fx[f, 20:24] = jnp.zeros((4, 16, 128), F32)
        for i in range(fy.shape[1]):
            fy[f, i, 0:8] = jnp.zeros((8, 128), F32)
            fy[f, i, 24:32] = jnp.zeros((8, 128), F32)

    lax.fori_loop(0, 16, cell_step, 0, unroll=2)
    for h in range(2):
        values = [v[8 * h : 8 * h + 8].reshape(128, 128) for v in (uv.at[0], uv.at[1], uv.at[2], tv, lv)]
        for k, value in enumerate(values):
            high, low = split(value)
            table[k * 128 : (k + 1) * 128, h * 128 : h * 128 + 128] = high
            table[k * 128 : (k + 1) * 128, 256 + h * 128 : 384 + h * 128] = low

    pl.when(first_plane)(meet_and_send)

    def place(values, row):
        high, low = values
        ns[row * ROWS : (row + 1) * ROWS, 0:128] = high
        ns[row * ROWS : (row + 1) * ROWS, 128:256] = low

    for k in range(5):
        place(split(s5[k]), k)
    for k, ids in ((5, new_cell[...]), (6, cell[...])):
        upper = lax.shift_left(lax.shift_right_logical(ids, 8), 8)
        place((upper.astype(F32).astype(BF16), (ids & 255).astype(F32).astype(BF16)), k)
    leaving = 4 * CAP
    entry = lax.broadcasted_iota(I32, (1, CAP), 1)
    picked = jnp.concatenate([lists[r : r + 1, :] for r in range(4)], 1)
    valid = [entry < counts[0:1, 1 + r : 2 + r] for r in range(4)]
    row_mask = lax.broadcasted_iota(I32, (ROWS, leaving), 0) == lax.shift_right_logical(picked, 7)
    lane_hot = jnp.where(
        lax.broadcasted_iota(I32, (128, leaving), 0) == (picked & 127), 1.0, 0.0
    ).astype(BF16)
    row_hot = jnp.where(row_mask & jnp.concatenate(valid, 1), 1.0, 0.0).astype(BF16)
    departed = lax.dot_general(
        row_hot, lane_hot, (((1,), (1,)), ((), ())), preferred_element_type=F32
    )
    rows = jnp.dot(ns[...], jnp.concatenate([lane_hot, lane_hot], 0), preferred_element_type=F32)
    got = [
        jnp.sum(jnp.where(row_mask, rows[k * ROWS : (k + 1) * ROWS], 0.0), axis=0, keepdims=True)
        for k in range(7)
    ]
    column, row = cell_place(got[6].astype(I32))
    hot = jnp.where(
        lax.broadcasted_iota(I32, (256, leaving), 0) == column, 1.0, 0.0
    ).astype(BF16)
    rows = jnp.dot(table[...], jnp.concatenate([hot, hot], 0), preferred_element_type=F32)
    row_mask = lax.broadcasted_iota(I32, (128, leaving), 0) == row
    around = [
        jnp.sum(jnp.where(row_mask, rows[k * 128 : (k + 1) * 128], 0.0), axis=0, keepdims=True)
        for k in range(5)
    ]
    moved = advance(got[0], got[1], got[2:5], around, cube_root(got[0]))
    for r in range(4):
        lanes = slice(r * CAP, (r + 1) * CAP)
        for k in range(5):
            msg[r, k : k + 1, :] = jnp.where(valid[r], moved[k][:, lanes], 0.0)
        msg[r, 5:6, :] = jnp.where(valid[r], got[5][:, lanes], -1.0)
        msg[r, 6:8, :] = jnp.zeros((2, CAP), F32)
        copy = pltpu.make_async_remote_copy(
            src_ref=msg.at[r],
            dst_ref=arr.at[r],
            send_sem=send_sem.at[8 + r],
            recv_sem=recv_sem.at[8 + r],
            device_id=targets[r],
            device_id_type=MESH,
        )
        copy.start()
        sends.append(copy)
    send_faces(1)

    per = TILE // 128
    planes = 16 * per // ROWS
    column_ids = lax.broadcasted_iota(I32, (256, 128), 0)
    row_ids = lax.broadcasted_iota(I32, (128, 128), 0)
    dep[...] = jnp.zeros_like(dep)

    def droplet_step(t, carry):
        hots = []
        masks = []
        for j in range(per):
            c = cell[pl.ds(t * per + j, 1), :]
            column, row = cell_place(c)
            hots.append(jnp.where(column_ids == column, 1.0, 0.0).astype(BF16))
            masks.append(row_ids == row)
        for j in range(0, per, 2):
            hot = jnp.concatenate(hots[j : j + 2], 1)
            rows = jnp.dot(
                table[...], jnp.concatenate([hot, hot], 0), preferred_element_type=F32
            )
            mask = jnp.concatenate(masks[j : j + 2], 1)
            for k in range(5):
                got = jnp.sum(
                    jnp.where(mask, rows[k * 128 : (k + 1) * 128], 0.0), axis=0, keepdims=True
                )
                gas[k, pl.ds(t * per + j, 1), :] = got[:, :128]
                gas[k, pl.ds(t * per + j + 1, 1), :] = got[:, 128:]
        lefts = []
        for k in range(5):
            parts = [
                jnp.where(masks[j], sv[half + k, pl.ds(t * per + j, 1), :], 0.0).astype(BF16)
                for half in (0, 5)
                for j in range(per)
            ]
            lefts.append(jnp.concatenate(parts, 1))
        sums = lax.dot_general(
            jnp.concatenate(lefts, 0),
            jnp.concatenate(hots + hots, 1),
            (((1,), (1,)), ((), ())),
            preferred_element_type=F32,
        )
        for k in range(5):
            dep[k] += sums[k * 128 : (k + 1) * 128]
        for i in range(planes):
            x = t * planes + i
            uy = uv[1, x]
            uz = uv[2, x]
            p = pv[x]
            for f in range(N_F):
                value = fv[f, x]
                fy[f, i, 8:24] = flux(f, 1, value, uy, p)
                fz = flux(f, 2, value, uz, p)
                total = None
                for k in range(4):
                    term = STENCIL[k] * (
                        (fx[f, x + 5 + k] - fx[f, x + 3 - k])
                        + (fy[f, i, 9 + k : 25 + k] - fy[f, i, 7 - k : 23 - k])
                        + (pltpu.roll(fz, 127 - k, 1) - pltpu.roll(fz, k + 1, 1))
                    )
                    total = term if total is None else total + term
                if SHARES[f] != 0.0:
                    part[f, x] = SHARES[f] * wv[x] - total
                else:
                    part[f, x] = -total
        return carry

    lax.fori_loop(0, ROWS // per, droplet_step, 0)

    new_state = advance(mass, theta, [s5[2], s5[3], s5[4]], [gas[k] for k in range(5)], size)
    staying = live & (departed == 0.0)
    cells[0:ROWS, :] = jnp.where(staying, new_cell[...], -1)
    for k in range(5):
        gas[k] = jnp.where(staying, new_state[k], 0.0)
    for i in range(ROWS):
        for k in range(5):
            drops[k : k + 1, i * 128 : (i + 1) * 128] = gas[k, i : i + 1, :]

    def deposit_step(x, carry):
        u = [uv[a, x] for a in range(3)]
        log = lv[x]
        rows = pl.ds(pl.multiple_of(lax.rem(x, 8) * 16, 16), 16)
        lanes = pl.ds(pl.multiple_of(lax.div(x, 8) * 128, 128), 128)
        sums = [dep[k, rows, lanes] for k in range(5)]
        evap = log * sums[0]
        part[0, x] += evap
        part[5, x] += evap
        for a in range(3):
            part[1 + a, x] += (log + 0.8) * sums[1 + a] - 0.8 * u[a] * sums[0]
        part[4, x] += (log + 0.6) * sums[4] - 0.6 * tv[x] * sums[0]
        return carry

    lax.fori_loop(0, 16, deposit_step, 0, unroll=2)
    for copy in sends[8:]:
        copy.wait()
    for r in range(4):
        drops[:, SLOTS + CAP * r : SLOTS + CAP * (r + 1)] = arr[r, 0:5, :]
        for j in range(2):
            row = ROWS + 2 * r + j
            cells[row : row + 1, :] = arr[r, 5:6, 128 * j : 128 * j + 128].astype(I32)
    for copy in sends[:8]:
        copy.wait()


def edge_kernel(
    part, xh, yh, drops, cells,
    out_h, drops_h, cells_h,
    out, ux, px, uy, py, fy, sem,
):
    copies = [
        pltpu.make_async_copy(drops, drops_h, sem.at[N_F]),
        pltpu.make_async_copy(cells, cells_h, sem.at[N_F + 1]),
    ]
    for copy in copies:
        copy.start()

    def cell_step(x, carry):
        _, u, _, p = primitives([yh[f, x] for f in range(5)])
        uy[x] = u[1]
        py[x] = p
        return carry

    lax.fori_loop(0, 16, cell_step, 0, unroll=16)
    for s in range(2):
        for i in range(4):
            _, u, _, p = primitives([xh[s, f, i] for f in range(5)])
            ux[s, i] = u[0]
            px[s, i] = p

    for x in range(16):
        fy[x, 8:24] = jnp.zeros((16, 128), F32)
    for f in range(N_F):
        low_x = [flux(f, 0, xh[0, f, i], ux[0, i], px[0, i]) for i in range(4)]
        high_x = [flux(f, 0, xh[1, f, i], ux[1, i], px[1, i]) for i in range(4)]
        for x in range(16):
            edge = flux(f, 1, yh[f, x], uy[x], py[x])
            fy[x, 0:8] = edge
            fy[x, 24:32] = edge
        for x in range(16):
            base = part[f, x]
            if x < 4:
                for k in range(x, 4):
                    base = base + STENCIL[k] * low_x[3 + x - k]
            if x >= 12:
                for k in range(15 - x, 4):
                    base = base - STENCIL[k] * high_x[k - (15 - x)]
            low = None
            high = None
            for k in range(4):
                term = STENCIL[k] * fy[x, 7 - k : 15 - k]
                low = term if low is None else low + term
                term = STENCIL[k] * fy[x, 17 + k : 25 + k]
                high = term if high is None else high + term
            out[f, x, 0:8] = base[0:8] + low
            out[f, x, 8:16] = base[8:16] - high
        copy = pltpu.make_async_copy(out.at[f], out_h.at[f], sem.at[f])
        copy.start()
        copies.append(copy)
    for copy in copies:
        copy.wait()


def shape(dims, dtype=F32):
    return jax.ShapeDtypeStruct(dims, dtype)


def per_device(n_gx, n_gy, fields, state, cell, new_cell, lists, counts):
    n_f, n_x, n_y, n_z = fields.shape
    vmem = pl.BlockSpec(memory_space=pltpu.VMEM)
    hbm = pl.BlockSpec(memory_space=pltpu.HBM)
    cube = (n_x, n_y, n_z)
    part, xh, yh, drops, cells = pl.pallas_call(
        functools.partial(droplet_kernel, n_gx, n_gy),
        out_shape=(
            shape((n_f,) + cube),
            shape((2, n_f, 4, n_y, n_z)),
            shape((n_f, n_x, 2, 4, n_z)),
            shape((5, SLOTS + 4 * CAP)),
            shape((ROWS + 8, 128), I32),
        ),
        in_specs=[hbm] * 7,
        out_specs=(vmem,) * 5,
        scratch_shapes=[
            pltpu.VMEM((n_f,) + cube, F32),
            pltpu.VMEM((ROWS, 128), I32),
            pltpu.VMEM((ROWS, 128), I32),
            pltpu.VMEM((4, CAP), I32),
            pltpu.VMEM((1, 5), I32),
            pltpu.VMEM((5, SLOTS), F32),
            pltpu.VMEM((640, 512), BF16),
            pltpu.VMEM((5, ROWS, 128), F32),
            pltpu.VMEM((10, ROWS, 128), F32),
            pltpu.VMEM((5, ROWS, 128), F32),
            pltpu.VMEM((7 * ROWS, 256), BF16),
            pltpu.VMEM((4, 8, CAP), F32),
            pltpu.VMEM((4, 8, CAP), F32),
            pltpu.VMEM((5, 128, 256), F32),
            pltpu.VMEM((3,) + cube, F32),
            pltpu.VMEM(cube, F32),
            pltpu.VMEM(cube, F32),
            pltpu.VMEM(cube, F32),
            pltpu.VMEM(cube, F32),
            pltpu.VMEM((n_f, n_x + 8, n_y, n_z), F32),
            pltpu.VMEM((n_f, n_x * TILE // SLOTS, n_y + 16, n_z), F32),
            pltpu.SemaphoreType.DMA((6,)),
            pltpu.SemaphoreType.DMA((12,)),
            pltpu.SemaphoreType.DMA((12,)),
        ],
        compiler_params=pltpu.CompilerParams(
            collective_id=0, has_side_effects=True, vmem_limit_bytes=36 << 20
        ),
        name="droplets",
    )(
        *(
            pltpu.with_memory_space_constraint(a, pltpu.HBM)
            for a in (
                fields,
                fields.reshape(n_f, n_x, n_y // 4, 4, n_z),
                state,
                cell.reshape(ROWS, 128),
                new_cell.reshape(ROWS, 128),
                lists,
                counts,
            )
        )
    )
    out, drops, cells = pl.pallas_call(
        edge_kernel,
        out_shape=(
            shape((n_f,) + cube),
            shape((5, SLOTS + 4 * CAP)),
            shape((ROWS + 8, 128), I32),
        ),
        in_specs=[vmem] * 5,
        out_specs=(hbm,) * 3,
        scratch_shapes=[
            pltpu.VMEM((n_f,) + cube, F32),
            pltpu.VMEM((2, 4, n_y, n_z), F32),
            pltpu.VMEM((2, 4, n_y, n_z), F32),
            pltpu.VMEM((n_x, 8, n_z), F32),
            pltpu.VMEM((n_x, 8, n_z), F32),
            pltpu.VMEM((n_x, n_y + 16, n_z), F32),
            pltpu.SemaphoreType.DMA((n_f + 2,)),
        ],
        compiler_params=pltpu.CompilerParams(vmem_limit_bytes=24 << 20),
        name="edges",
    )(part, xh, yh.reshape(n_f, n_x, 8, n_z), drops, cells)
    return out, drops, cells.reshape(-1)


def solution(mesh):
    placed = (
        P(None, "gx", "gy", None),
        P(None, ("gx", "gy")),
        P(("gx", "gy")),
        P(("gx", "gy")),
        P(("gx", "gy"), None),
        P(("gx", "gy"), None),
    )
    return jax.shard_map(
        functools.partial(per_device, mesh.shape["gx"], mesh.shape["gy"]),
        mesh=mesh,
        in_specs=placed,
        out_specs=(P(None, "gx", "gy", None), P(None, ("gx", "gy")), P(("gx", "gy"))),
        check_vma=False,
    )
```
